512 devices in a mesh: subset: 8 (over x, z_lo), tile: 64 (over y, z_hi, core).
Axes of the slice: x: 4, y: 8, z: 8 (z_hi: 4, z_lo: 2; z = z_hi * 2 + z_lo), core: 2. Of those that a mesh axis runs over, the one named last changes fastest.
Arguments:
- images: float32 [256, 131072], P('subset', 'tile'), may hold values from 0.5 to 2
- system_tiles: bfloat16 [8, 2048, 128, 128], P('subset', 'tile'), may hold values from 5.197525e-05 to 0.0025939941
- tile_vox: int32 [8, 2048], P('subset', 'tile'), may hold values from 0 to 15, as said below
- tile_ray: int32 [8, 2048], P('subset', 'tile'), may hold values from 0 to 63, as said below
- live_blocks: int32 [8, 64], P('subset', 'tile'), may hold values from 1 to 1, as said below
- counts: int32 [8, 256, 8192], P('subset', None, 'tile'), may hold values from 1 to 7
Outputs:
- updated: float32 [256, 131072], P('subset', 'tile')
The draws below stay inside these ranges and needn't reach their ends.
Inputs may be any that keep to these rules, and one draw needn't show every extreme that they name: `tile_vox`: within each image tile and subset, the first 16 tile slots name every voxel block of that image tile once. `tile_ray`: in each subset every ray block is named by one of the first 1 tile slots of some image tile. `live_blocks`: slots in use are the first ones of an image tile; in every draw some image tile uses all of its blocks.
All inputs are finite; a program needn't handle non-finite values.
Results may differ from the reference program's by a relative error of at most 0.00063.
Values may be sent and summed in bfloat16 or wider, within the bound.
A program may use at most 64 MiB of HBM per device.

```python
import math
import jax
import jax.numpy as jnp
from jax import lax

BLOCK = 128
VB_DEV = 16
RB_DEV = 1
TILES_DEV = 32
TILE_GROUP = 32
FP = 32
ROUNDS = 4
SUBSETS = 8
TILE_DEVS = 64
RB_TOTAL = 64
VOXELS = 131072
FRAMES = 256
TILES_ALL = 2048
N_SUBSET = 8
N_TILE = 64


def draw_tile_vox(key, part):
    first_key, other_key = jax.random.split(jax.random.fold_in(key, 11))
    key_list = jax.random.split(first_key, SUBSETS * TILE_DEVS)
    leading = jax.vmap(lambda single: jax.random.permutation(single, VB_DEV))(key_list)
    remaining = jax.random.randint(other_key, (SUBSETS * TILE_DEVS, TILES_DEV - VB_DEV), 0, VB_DEV)
    joined = jnp.concatenate([leading.astype(jnp.int32), remaining.astype(jnp.int32)], axis=1)
    return joined.reshape(SUBSETS, TILE_DEVS * TILES_DEV)


def draw_tile_ray(key, part):
    first_key, other_key = jax.random.split(jax.random.fold_in(key, 23))
    key_list = jax.random.split(first_key, SUBSETS)
    leading = jax.vmap(lambda single: jax.random.permutation(single, RB_TOTAL))(key_list)
    leading = leading.reshape(SUBSETS, TILE_DEVS, RB_DEV).astype(jnp.int32)
    remaining = jax.random.randint(other_key, (SUBSETS, TILE_DEVS, TILES_DEV - RB_DEV), 0, RB_TOTAL)
    joined = jnp.concatenate([leading, remaining.astype(jnp.int32)], axis=2)
    return joined.reshape(SUBSETS, TILE_DEVS * TILES_DEV)


def draw_live_blocks(key, part):
    first_key, other_key = jax.random.split(jax.random.fold_in(key, 37))
    largest = TILES_DEV // TILE_GROUP
    lowest = max(1, largest // 2)
    filled = jax.random.randint(first_key, (SUBSETS * TILE_DEVS,), lowest, largest + 1).astype(jnp.int32)
    picked = jax.random.randint(other_key, (), 0, SUBSETS * TILE_DEVS)
    filled = filled.at[picked].set(largest)
    return filled.astype(jnp.int32).reshape(SUBSETS, TILE_DEVS)


def set_ends(result, own_key, least, top_value):
    longest = result.shape.index(max(result.shape))
    spots = []
    for shift in (0, 1):
        where = [jax.random.randint(jax.random.fold_in(own_key, axis), (), 0, length) for axis, length in enumerate(result.shape)]
        where[longest] = (where[longest] + shift) % result.shape[longest]
        spots.append(tuple(where))
    return result.at[spots[0]].set(least).at[spots[1]].set(top_value)


def steps_of(stream_key, extent, shards, least, high):
    def one(axis_at, shards_of):
        heights = jax.random.uniform(jax.random.fold_in(jax.random.fold_in(stream_key, 6), axis_at), (shards_of,), jnp.float32, least / len(shards), high / len(shards))
        return jnp.repeat(jnp.exp(heights), extent[axis_at] // shards_of).reshape((-1,) + (1,) * (len(extent) - axis_at - 1))

    loudness = one(*shards[0])
    for cut in shards[1:]:
        loudness = loudness * one(*cut)
    return loudness


def setup_inputs(seed: int = 0) -> dict:
    splits = jax.random.split(jax.random.key(seed), 7)
    images = jnp.clip(jnp.exp(math.log(2.0) - 1.3862944 * jax.random.uniform(splits[0], (FRAMES, VOXELS), jnp.float32) ** steps_of(splits[0], (FRAMES, VOXELS), ((0, 8), (1, 64)), -0.2, 0.2)), 0.5, 2.0)
    system_tiles = jnp.clip(jnp.exp(math.log(0.0025939941) - 3.9101865 * jax.random.uniform(splits[1], (SUBSETS, TILES_ALL, BLOCK, BLOCK), jnp.float32) ** steps_of(splits[1], (SUBSETS, TILES_ALL, BLOCK, BLOCK), ((0, 8), (1, 64)), -0.2, 0.2)), 5.1975250244140625e-05, 0.0025939941).astype(jnp.bfloat16)
    tile_vox = draw_tile_vox(jax.random.fold_in(splits[6], 71), 0)
    tile_ray = draw_tile_ray(jax.random.fold_in(splits[6], 71), 0)
    live_blocks = draw_live_blocks(jax.random.fold_in(splits[6], 71), 0)
    counts = set_ends(jax.random.randint(splits[5], (SUBSETS, FRAMES, RB_TOTAL * BLOCK), 1, 8), jax.random.fold_in(splits[5], 1), 1, 7).astype(jnp.int32)
    return {"images": images, "system_tiles": system_tiles, "tile_vox": tile_vox, "tile_ray": tile_ray, "live_blocks": live_blocks, "counts": counts}


HIGHEST = lax.Precision.HIGHEST


def group_pass(panel, system_tiles, tile_vox, tile_ray, live_blocks, counts_now):
    tile_set = system_tiles.reshape(N_TILE, TILES_DEV, BLOCK, BLOCK)
    voxel_index = tile_vox.reshape(N_TILE, TILES_DEV).astype(jnp.int32)
    ray_index = tile_ray.reshape(N_TILE, TILES_DEV).astype(jnp.int32)
    panel_tiles = panel.reshape(FP, N_TILE, VB_DEV, BLOCK).transpose(1, 0, 2, 3)
    slot_groups = jnp.arange(TILES_DEV, dtype=jnp.int32) // TILE_GROUP
    ray_ids = jnp.arange(RB_TOTAL, dtype=jnp.int32)
    vox_ids = jnp.arange(VB_DEV, dtype=jnp.int32)

    def forward(running, entry):
        panel_dev, tiles_dev, vox_dev, ray_dev, live_dev = entry
        tile_mask = (slot_groups < live_dev).astype(jnp.float32)
        lowered = panel_dev.astype(jnp.bfloat16)
        chosen = jnp.take(lowered, vox_dev, axis=1).astype(jnp.float32)
        contrib = jnp.einsum('ftv,trv->tfr', chosen, tiles_dev.astype(jnp.float32))
        contrib = contrib * tile_mask[:, None, None]
        onehot = (ray_dev[None, :] == ray_ids[:, None]).astype(jnp.float32)
        return running + jnp.einsum('bt,tfr->fbr', onehot, contrib, precision=HIGHEST), None

    projected, _ = lax.scan(forward, jnp.zeros((FP, RB_TOTAL, BLOCK), jnp.float32),
                            (panel_tiles, tile_set, voxel_index, ray_index, live_blocks))
    ratios = (counts_now.astype(jnp.float32).reshape(FP, RB_TOTAL, BLOCK) / projected).astype(jnp.bfloat16)

    def backward(entry):
        panel_dev, tiles_dev, vox_dev, ray_dev, live_dev = entry
        tile_mask = (slot_groups < live_dev).astype(jnp.float32)
        tiles_wide = tiles_dev.astype(jnp.float32)
        chosen = jnp.take(ratios, ray_dev, axis=1).astype(jnp.float32)
        contrib = jnp.einsum('ftr,trv->tfv', chosen, tiles_wide) * tile_mask[:, None, None]
        onehot = (vox_dev[None, :] == vox_ids[:, None]).astype(jnp.float32)
        back_sum = jnp.einsum('ct,tfv->fcv', onehot, contrib, precision=HIGHEST)
        column = jnp.sum(tiles_wide, axis=1) * tile_mask[:, None]
        sensitivity = jnp.einsum('ct,tv->cv', onehot, column, precision=HIGHEST)
        return panel_dev * back_sum / sensitivity[None]

    updated = lax.map(backward, (panel_tiles, tile_set, voxel_index, ray_index, live_blocks))
    return updated.transpose(1, 0, 2, 3).reshape(FP, VOXELS)


def reference(images, system_tiles, tile_vox, tile_ray, live_blocks, counts):
    held = images.reshape(N_SUBSET, FP, VOXELS)
    group_ids = jnp.arange(N_SUBSET, dtype=jnp.int32)
    measured = counts.reshape(N_SUBSET, N_SUBSET, FP, RB_TOTAL * BLOCK)
    stepper = jax.vmap(group_pass)
    for round_index in range(ROUNDS):
        panel_ids = ((group_ids - round_index) % N_SUBSET).astype(jnp.int32)
        counts_now = measured[group_ids, panel_ids]
        held = stepper(held, system_tiles, tile_vox, tile_ray, live_blocks, counts_now)
        if round_index + 1 < ROUNDS:
            held = jnp.roll(held, 1, axis=0)
    return held.reshape(FRAMES, VOXELS)
```

```python
import functools

import jax
import jax.numpy as jnp
from jax import lax
from jax.experimental import pallas as pl
from jax.experimental.pallas import tpu as pltpu
from jax.sharding import PartitionSpec as P

TILE_GROUP = 32
ROUNDS = 4
SUBSETS = 8
SLOTS = 32
VOX = 16
RAYS = 64
B = 128
NY = 8
NZ = 4
FP = 32
HALVES = 2
F = FP // HALVES
OWN = RAYS // 2

PREV_R, PREV_V, VOX_OF, RATIO_OF, LAST_R, LAST_V, TABLE = 0, 32, 64, 96, 128, 192, 256

f32 = jnp.float32
bf16 = jnp.bfloat16


def prepare(vox_ref, ray_ref, live_ref, table_ref):
    core = lax.rem(lax.axis_index("tile"), 2)
    live = live_ref[0, 0]
    for i in range(TABLE):
        table_ref[i] = SLOTS
    for t in range(SLOTS):
        vox, ray = vox_ref[0, t], ray_ref[0, t]
        table_ref[VOX_OF + t] = vox
        table_ref[RATIO_OF + t] = jnp.where(lax.rem(ray, 2) == core, 0, OWN) + lax.div(ray, 2)
        alive = t // TILE_GROUP < live
        for last, prev, block in ((LAST_R, PREV_R, ray), (LAST_V, PREV_V, vox)):
            before = table_ref[last + block]
            table_ref[prev + t] = before
            table_ref[last + block] = jnp.where(alive, t, before)


def fused(
    table, images, tiles, counts, out,
    low_0a, low_0b, low_1a, low_1b, low_2a, low_2b, low_3a, low_3b,
    rest, send_high, send_low, acc_a, acc_b, acc_back, inverse,
    send_c, recv_c, send_y, recv_y, send_z, recv_z, ratio_a, ratio_b, cnt,
    s_c, r_c, s_y, r_y, s_z, r_z, s_g, r_g, s_p, r_p, s_h, r_h, s_l, r_l, s_n, r_n,
):
    low = ((low_0a, low_0b), (low_1a, low_1b), (low_2a, low_2b), (low_3a, low_3b))
    acc = (acc_a, acc_b)
    ratio = (ratio_a, ratio_b)
    subset = lax.axis_index("subset")
    tile = lax.axis_index("tile")
    core = lax.rem(tile, 2)
    z = lax.rem(lax.div(tile, 2), NZ)
    y = lax.div(tile, 2 * NZ)

    def at(y_of, z_of, c_of):
        return {"tile": (y_of * NZ + z_of) * 2 + c_of}

    partner = at(y, z, 1 - core)
    y_of = [None] + [lax.rem(y + k, NY) for k in range(1, NY)]
    y_peers = [None] + [at(y_of[k], z, core) for k in range(1, NY)]
    z_peers = [None] + [at(y, lax.rem(z + k, NZ), core) for k in range(1, NZ)]
    ahead = {"subset": lax.rem(subset + 1, SUBSETS)}
    behind = {"subset": lax.rem(subset + SUBSETS - 1, SUBSETS)}
    everyone = [partner] + y_peers[1:] + z_peers[1:] + [ahead, behind]
    far_first_y = (4, 3, 5, 2, 6, 1, 7)
    far_first_z = (2, 1, 3)

    barrier = pltpu.get_barrier_semaphore()
    for peer in everyone:
        pl.semaphore_signal(barrier, inc=1, device_id=peer, device_id_type=pl.DeviceIdType.MESH)

    def remote(src, dst, send, recv, peer):
        return pltpu.make_async_remote_copy(
            src_ref=src, dst_ref=dst, send_sem=send, recv_sem=recv,
            device_id=peer, device_id_type=pl.DeviceIdType.MESH,
        )

    def await_bytes(ref, sem):
        pltpu.make_async_copy(ref, ref, sem).wait()

    def frames(h):
        return slice(h * F, (h + 1) * F)

    for h in range(HALVES):
        acc[h][SLOTS] = jnp.zeros((F, B), f32)
        for v in range(VOX):
            low[0][h][v] = images[frames(h), v * B : (v + 1) * B].astype(bf16)
    acc_back[SLOTS] = jnp.zeros((F, B), f32)
    for r in range(ROUNDS):
        panel = lax.rem(subset - r + SUBSETS, SUBSETS)
        rows = pl.ds(pl.multiple_of(panel * FP, FP), FP)
        cnt[z, r] = counts[0, rows, :].astype(f32).astype(bf16)

    def project(r, h):
        for t in range(SLOTS):
            chosen = low[r][h][table[VOX_OF + t]]
            product = lax.dot_general(
                chosen, tiles[0, t], (((1,), (1,)), ((), ())), preferred_element_type=f32
            )
            acc[h][t] = product + acc[h][table[PREV_R + t]]
        for j in range(OWN):
            send_c[h, j] = acc[h][table[LAST_R + 2 * j + 1 - core]].astype(bf16)

    def backproject(h):
        for t in range(SLOTS):
            product = jnp.dot(
                ratio[h][table[RATIO_OF + t]], tiles[0, t], preferred_element_type=f32
            )
            acc_back[t] = product + acc_back[table[PREV_V + t]]

    for r in range(ROUNDS):
        p = r % 2
        last = r + 1 == ROUNDS
        for h in range(HALVES):
            if r > 0:
                await_bytes(low[r][h], r_h.at[r - 1, h])
                await_bytes(send_c.at[h], s_c.at[h])
            project(r, h)
            if r == 0 and h == 0:
                pl.semaphore_wait(barrier, len(everyone))
                for k in far_first_z:
                    remote(cnt.at[z], cnt.at[z], s_n, r_n, z_peers[k]).start()
            remote(send_c.at[h], recv_c.at[h], s_c.at[h], r_c.at[h], partner).start()
        for h in range(HALVES):
            await_bytes(recv_c.at[h], r_c.at[h])
            if r > 0:
                await_bytes(recv_y.at[h], s_y.at[h])
                await_bytes(ratio[h].at[pl.ds(0, OWN)], s_p.at[h])
            for j in range(OWN):
                own = acc[h][table[LAST_R + 2 * j + core]]
                send_y[h, j] = (own + recv_c[h, j].astype(f32)).astype(bf16)
            for k in far_first_y:
                remote(
                    send_y.at[h, pl.ds(y_of[k] * NZ, NZ)], recv_y.at[h, k - 1],
                    s_y.at[h], r_y.at[h], y_peers[k],
                ).start()
        if r == 0:
            ones = jnp.ones((F, B), bf16)
            for t in range(SLOTS):
                column = jnp.dot(ones, tiles[0, t], preferred_element_type=f32)
                acc_back[t] = column + acc_back[table[PREV_V + t]]
            for v in range(VOX):
                inverse[v] = 1.0 / acc_back[table[LAST_V + v]]
            await_bytes(cnt.at[pl.ds(0, NZ - 1)], r_n)
        for h in range(HALVES):
            await_bytes(recv_y.at[h], r_y.at[h])
            if r > 1:
                await_bytes(recv_z.at[p, h], s_z.at[p, h])
            for b in range(NZ):
                total = send_y[h, y * NZ + b].astype(f32)
                for k in range(NY - 1):
                    total = total + recv_y[h, k, b].astype(f32)
                send_z[p, h, b] = total.astype(bf16)
            for k in far_first_z:
                remote(
                    send_z.at[p, h], recv_z.at[p, h, k - 1], s_z.at[p, h], r_z.at[p, h], z_peers[k]
                ).start()
        for h in range(HALVES):
            await_bytes(recv_z.at[p, h], r_z.at[p, h])
            if r > 0:
                await_bytes(ratio[h].at[pl.ds(0, NZ * (NY - 1))], s_g.at[h])
            for b in range(NZ):
                even = send_z[p, h, b].astype(f32) + recv_z[p, h, 1, b].astype(f32)
                odd = recv_z[p, h, 0, b].astype(f32) + recv_z[p, h, 2, b].astype(f32)
                measured = cnt[b, r, frames(h), :].astype(f32)
                ratio[h][y * NZ + b] = (measured / (even + odd)).astype(bf16)
            mine = ratio[h].at[pl.ds(y * NZ, NZ)]
            for k in far_first_y:
                remote(mine, mine, s_g.at[h], r_g.at[h], y_peers[k]).start()
        for h in range(HALVES):
            await_bytes(ratio[h].at[pl.ds(0, NZ * (NY - 1))], r_g.at[h])
            remote(
                ratio[h].at[pl.ds(0, OWN)], ratio[h].at[pl.ds(OWN, OWN)], s_p.at[h], r_p.at[h], partner
            ).start()
        for h in range(HALVES):
            await_bytes(ratio[h].at[pl.ds(OWN, OWN)], r_p.at[h])
            backproject(h)
            if r > 0:
                await_bytes(rest.at[r - 1, h], r_l.at[r - 1, h])
                if not last:
                    await_bytes(send_high.at[h], s_h.at[r - 1, h])
                    await_bytes(send_low.at[h], s_l.at[r - 1, h])
            for v in range(VOX):
                if r == 0:
                    held = images[frames(h), v * B : (v + 1) * B]
                else:
                    held = low[r][h][v].astype(f32) + rest[r - 1, h, v].astype(f32)
                held = held * acc_back[table[LAST_V + v]] * inverse[v]
                if last:
                    out[frames(h), v * B : (v + 1) * B] = held
                else:
                    high = held.astype(bf16)
                    send_high[h, v] = high
                    send_low[h, v] = (held - high.astype(f32)).astype(bf16)
            if not last:
                remote(send_high.at[h], low[r + 1][h], s_h.at[r, h], r_h.at[r, h], ahead).start()
                remote(send_low.at[h], rest.at[r, h], s_l.at[r, h], r_l.at[r, h], ahead).start()

    await_bytes(cnt.at[pl.ds(0, NZ - 1)], s_n)
    for h in range(HALVES):
        await_bytes(send_c.at[h], s_c.at[h])
        await_bytes(recv_y.at[h], s_y.at[h])
        for p in range(2):
            await_bytes(recv_z.at[p, h], s_z.at[p, h])
        await_bytes(ratio[h].at[pl.ds(0, NZ * (NY - 1))], s_g.at[h])
        await_bytes(ratio[h].at[pl.ds(0, OWN)], s_p.at[h])
        await_bytes(send_high.at[h], s_h.at[ROUNDS - 2, h])
        await_bytes(send_low.at[h], s_l.at[ROUNDS - 2, h])


def shards(images, system_tiles, tile_vox, tile_ray, live_blocks, counts):
    smem = pl.BlockSpec(memory_space=pltpu.SMEM)
    vmem = pl.BlockSpec(memory_space=pltpu.VMEM)
    table = pl.pallas_call(
        prepare,
        out_shape=jax.ShapeDtypeStruct((TABLE,), jnp.int32),
        in_specs=[smem] * 3,
        out_specs=smem,
        name="prepare",
    )(tile_vox, tile_ray, live_blocks)
    half = pltpu.VMEM((VOX, F, B), bf16)
    dma = pltpu.SemaphoreType.DMA
    return pl.pallas_call(
        fused,
        out_shape=jax.ShapeDtypeStruct(images.shape, f32),
        in_specs=[smem, vmem, vmem, vmem],
        out_specs=vmem,
        scratch_shapes=[half] * (2 * ROUNDS)
        + [
            pltpu.VMEM((ROUNDS - 1, HALVES, VOX, F, B), bf16),
            pltpu.VMEM((HALVES, VOX, F, B), bf16),
            pltpu.VMEM((HALVES, VOX, F, B), bf16),
            pltpu.VMEM((SLOTS + 1, F, B), f32),
            pltpu.VMEM((SLOTS + 1, F, B), f32),
            pltpu.VMEM((SLOTS + 1, F, B), f32),
            pltpu.VMEM((VOX, F, B), f32),
            pltpu.VMEM((HALVES, OWN, F, B), bf16),
            pltpu.VMEM((HALVES, OWN, F, B), bf16),
            pltpu.VMEM((HALVES, OWN, F, B), bf16),
            pltpu.VMEM((HALVES, NY - 1, NZ, F, B), bf16),
            pltpu.VMEM((2, HALVES, NZ, F, B), bf16),
            pltpu.VMEM((2, HALVES, NZ - 1, NZ, F, B), bf16),
            pltpu.VMEM((RAYS, F, B), bf16),
            pltpu.VMEM((RAYS, F, B), bf16),
            pltpu.VMEM((NZ, ROUNDS, FP, B), bf16),
            dma((HALVES,)), dma((HALVES,)),
            dma((HALVES,)), dma((HALVES,)),
            dma((2, HALVES)), dma((2, HALVES)),
            dma((HALVES,)), dma((HALVES,)),
            dma((HALVES,)), dma((HALVES,)),
            dma((ROUNDS - 1, HALVES)), dma((ROUNDS - 1, HALVES)),
            dma((ROUNDS - 1, HALVES)), dma((ROUNDS - 1, HALVES)),
            dma, dma,
        ],
        compiler_params=pltpu.CompilerParams(collective_id=0, has_side_effects=True),
        name="fused",
    )(table, images, system_tiles, counts)


def solution(mesh):
    in_specs = (
        P("subset", "tile"),
        P("subset", "tile", None, None),
        P("subset", "tile"),
        P("subset", "tile"),
        P("subset", "tile"),
        P("subset", None, "tile"),
    )
    out_specs = P("subset", "tile")
    return jax.shard_map(shards, mesh=mesh, in_specs=in_specs, out_specs=out_specs, check_vma=False)
```

```python
import functools

import jax
import jax.numpy as jnp
from jax import lax
from jax.experimental import pallas as pl
from jax.experimental.pallas import tpu as pltpu
from jax.sharding import PartitionSpec as P

TILE_GROUP = 32
ROUNDS = 4
SUBSETS = 8
SLOTS = 32
VOX = 16
RAYS = 64
B = 128
NY = 8
NZ = 4
FP = 32
HALVES = 2
F = FP // HALVES
OWN = RAYS // 2

PREV_R, PREV_V, VOX_OF, RATIO_OF, LAST_R, LAST_V, TABLE = 0, 32, 64, 96, 128, 192, 256

f32 = jnp.float32
bf16 = jnp.bfloat16


def prepare(vox_ref, ray_ref, live_ref, table_ref):
    core = lax.rem(lax.axis_index("tile"), 2)
    live = live_ref[0, 0]
    for i in range(TABLE):
        table_ref[i] = SLOTS
    for t in range(SLOTS):
        vox, ray = vox_ref[0, t], ray_ref[0, t]
        table_ref[VOX_OF + t] = vox
        table_ref[RATIO_OF + t] = jnp.where(lax.rem(ray, 2) == core, 0, OWN) + lax.div(ray, 2)
        alive = t // TILE_GROUP < live
        for last, prev, block in ((LAST_R, PREV_R, ray), (LAST_V, PREV_V, vox)):
            before = table_ref[last + block]
            table_ref[prev + t] = before
            table_ref[last + block] = jnp.where(alive, t, before)


def fused(
    table, images, tiles, counts, out,
    low_0a, low_0b, low_1a, low_1b, low_2a, low_2b, low_3a, low_3b,
    rest, send_high, send_low, acc_a, acc_b, acc_back, inverse,
    send_c, recv_c, send_y, recv_y, send_z, recv_z, ratio_a, ratio_b, cnt,
    s_c, r_c, s_y, r_y, s_z, r_z, s_g, r_g, s_p, r_p, s_h, r_h, s_l, r_l, s_n, r_n,
):
    low = ((low_0a, low_0b), (low_1a, low_1b), (low_2a, low_2b), (low_3a, low_3b))
    acc = (acc_a, acc_b)
    ratio = (ratio_a, ratio_b)
    subset = lax.axis_index("subset")
    tile = lax.axis_index("tile")
    core = lax.rem(tile, 2)
    z = lax.rem(lax.div(tile, 2), NZ)
    y = lax.div(tile, 2 * NZ)

    def at(y_of, z_of, c_of):
        return {"tile": (y_of * NZ + z_of) * 2 + c_of}

    partner = at(y, z, 1 - core)
    y_of = [None] + [lax.rem(y + k, NY) for k in range(1, NY)]
    y_peers = [None] + [at(y_of[k], z, core) for k in range(1, NY)]
    z_peers = [None] + [at(y, lax.rem(z + k, NZ), core) for k in range(1, NZ)]
    ahead = {"subset": lax.rem(subset + 1, SUBSETS)}
    behind = {"subset": lax.rem(subset + SUBSETS - 1, SUBSETS)}
    everyone = [partner] + y_peers[1:] + z_peers[1:] + [ahead, behind]
    far_first_y = (4, 3, 5, 2, 6, 1, 7)
    far_first_z = (2, 1, 3)

    barrier = pltpu.get_barrier_semaphore()
    for peer in everyone:
        pl.semaphore_signal(barrier, inc=1, device_id=peer, device_id_type=pl.DeviceIdType.MESH)

    def remote(src, dst, send, recv, peer):
        return pltpu.make_async_remote_copy(
            src_ref=src, dst_ref=dst, send_sem=send, recv_sem=recv,
            device_id=peer, device_id_type=pl.DeviceIdType.MESH,
        )

    def await_bytes(ref, sem):
        pltpu.make_async_copy(ref, ref, sem).wait()

    def frames(h):
        return slice(h * F, (h + 1) * F)

    for h in range(HALVES):
        acc[h][SLOTS] = jnp.zeros((F, B), f32)
        for v in range(VOX):
            low[0][h][v] = images[frames(h), v * B : (v + 1) * B].astype(bf16)
    acc_back[SLOTS] = jnp.zeros((F, B), f32)
    for r in range(ROUNDS):
        panel = lax.rem(subset - r + SUBSETS, SUBSETS)
        rows = pl.ds(pl.multiple_of(panel * FP, FP), FP)
        cnt[z, r] = counts[0, rows, :].astype(f32).astype(bf16)

    def project(r, h):
        for t in range(SLOTS):
            chosen = low[r][h][table[VOX_OF + t]]
            product = lax.dot_general(
                chosen, tiles[0, t], (((1,), (1,)), ((), ())), preferred_element_type=f32
            )
            acc[h][t] = product + acc[h][table[PREV_R + t]]
        for j in range(OWN):
            send_c[h, j] = acc[h][table[LAST_R + 2 * j + 1 - core]].astype(bf16)

    def backproject(h):
        for t in range(SLOTS):
            product = jnp.dot(
                ratio[h][table[RATIO_OF + t]], tiles[0, t], preferred_element_type=f32
            )
            acc_back[t] = product + acc_back[table[PREV_V + t]]

    def stage_c(r, h):
        if r > 0:
            await_bytes(low[r][h], r_h.at[r - 1, h])
            await_bytes(send_c.at[h], s_c.at[h])
        project(r, h)
        if r == 0 and h == 0:
            pl.semaphore_wait(barrier, len(everyone))
        remote(send_c.at[h], recv_c.at[h], s_c.at[h], r_c.at[h], partner).start()

    def stage_y(r, h):
        await_bytes(recv_c.at[h], r_c.at[h])
        if r > 0:
            await_bytes(recv_y.at[h], s_y.at[h])
            await_bytes(ratio[h].at[pl.ds(0, OWN)], s_p.at[h])
        for j in range(OWN):
            own = acc[h][table[LAST_R + 2 * j + core]]
            send_y[h, j] = (own + recv_c[h, j].astype(f32)).astype(bf16)
        for k in far_first_y:
            remote(
                send_y.at[h, pl.ds(y_of[k] * NZ, NZ)], recv_y.at[h, k - 1],
                s_y.at[h], r_y.at[h], y_peers[k],
            ).start()

    def stage_z(r, h):
        p = r % 2
        await_bytes(recv_y.at[h], r_y.at[h])
        if r > 1:
            await_bytes(recv_z.at[p, h], s_z.at[p, h])
        for b in range(NZ):
            total = send_y[h, y * NZ + b].astype(f32)
            for k in range(NY - 1):
                total = total + recv_y[h, k, b].astype(f32)
            send_z[p, h, b] = total.astype(bf16)
        for k in far_first_z:
            remote(
                send_z.at[p, h], recv_z.at[p, h, k - 1], s_z.at[p, h], r_z.at[p, h], z_peers[k]
            ).start()

    def stage_g(r, h):
        p = r % 2
        await_bytes(recv_z.at[p, h], r_z.at[p, h])
        if r > 0:
            await_bytes(ratio[h].at[pl.ds(0, NZ * (NY - 1))], s_g.at[h])
        for b in range(NZ):
            even = send_z[p, h, b].astype(f32) + recv_z[p, h, 1, b].astype(f32)
            odd = recv_z[p, h, 0, b].astype(f32) + recv_z[p, h, 2, b].astype(f32)
            measured = cnt[b, r, frames(h), :].astype(f32)
            ratio[h][y * NZ + b] = (measured / (even + odd)).astype(bf16)
        mine = ratio[h].at[pl.ds(y * NZ, NZ)]
        for k in far_first_y:
            remote(mine, mine, s_g.at[h], r_g.at[h], y_peers[k]).start()

    def stage_p(h):
        await_bytes(ratio[h].at[pl.ds(0, NZ * (NY - 1))], r_g.at[h])
        remote(
            ratio[h].at[pl.ds(0, OWN)], ratio[h].at[pl.ds(OWN, OWN)], s_p.at[h], r_p.at[h], partner
        ).start()

    def stage_b(r, h):
        last = r + 1 == ROUNDS
        await_bytes(ratio[h].at[pl.ds(OWN, OWN)], r_p.at[h])
        backproject(h)
        if r > 0:
            await_bytes(rest.at[r - 1, h], r_l.at[r - 1, h])
            if not last:
                await_bytes(send_high.at[h], s_h.at[r - 1, h])
                await_bytes(send_low.at[h], s_l.at[r - 1, h])
        for v in range(VOX):
            if r == 0:
                held = images[frames(h), v * B : (v + 1) * B]
            else:
                held = low[r][h][v].astype(f32) + rest[r - 1, h, v].astype(f32)
            held = held * acc_back[table[LAST_V + v]] * inverse[v]
            if last:
                out[frames(h), v * B : (v + 1) * B] = held
            else:
                high = held.astype(bf16)
                send_high[h, v] = high
                send_low[h, v] = (held - high.astype(f32)).astype(bf16)
        if not last:
            remote(send_high.at[h], low[r + 1][h], s_h.at[r, h], r_h.at[r, h], ahead).start()
            remote(send_low.at[h], rest.at[r, h], s_l.at[r, h], r_l.at[r, h], ahead).start()

    def sensitivity():
        ones = jnp.ones((F, B), bf16)
        for t in range(SLOTS):
            column = jnp.dot(ones, tiles[0, t], preferred_element_type=f32)
            acc_back[t] = column + acc_back[table[PREV_V + t]]
        for v in range(VOX):
            inverse[v] = 1.0 / acc_back[table[LAST_V + v]]

    for r in range(ROUNDS):
        stage_c(r, 0)
        if r > 0:
            stage_b(r - 1, 1)
        stage_y(r, 0)
        stage_c(r, 1)
        stage_y(r, 1)
        if r == 0:
            for k in far_first_z:
                remote(cnt.at[z], cnt.at[z], s_n, r_n, z_peers[k]).start()
            sensitivity()
        stage_z(r, 0)
        stage_z(r, 1)
        if r == 0:
            await_bytes(cnt.at[pl.ds(0, NZ - 1)], r_n)
        stage_g(r, 0)
        stage_g(r, 1)
        stage_p(0)
        stage_b(r, 0)
        stage_p(1)
    stage_b(ROUNDS - 1, 1)

    await_bytes(cnt.at[pl.ds(0, NZ - 1)], s_n)
    for h in range(HALVES):
        await_bytes(send_c.at[h], s_c.at[h])
        await_bytes(recv_y.at[h], s_y.at[h])
        for p in range(2):
            await_bytes(recv_z.at[p, h], s_z.at[p, h])
        await_bytes(ratio[h].at[pl.ds(0, NZ * (NY - 1))], s_g.at[h])
        await_bytes(ratio[h].at[pl.ds(0, OWN)], s_p.at[h])
        await_bytes(send_high.at[h], s_h.at[ROUNDS - 2, h])
        await_bytes(send_low.at[h], s_l.at[ROUNDS - 2, h])


def shards(images, system_tiles, tile_vox, tile_ray, live_blocks, counts):
    smem = pl.BlockSpec(memory_space=pltpu.SMEM)
    vmem = pl.BlockSpec(memory_space=pltpu.VMEM)
    table = pl.pallas_call(
        prepare,
        out_shape=jax.ShapeDtypeStruct((TABLE,), jnp.int32),
        in_specs=[smem] * 3,
        out_specs=smem,
        name="prepare",
    )(tile_vox, tile_ray, live_blocks)
    half = pltpu.VMEM((VOX, F, B), bf16)
    dma = pltpu.SemaphoreType.DMA
    return pl.pallas_call(
        fused,
        out_shape=jax.ShapeDtypeStruct(images.shape, f32),
        in_specs=[smem, vmem, vmem, vmem],
        out_specs=vmem,
        scratch_shapes=[half] * (2 * ROUNDS)
        + [
            pltpu.VMEM((ROUNDS - 1, HALVES, VOX, F, B), bf16),
            pltpu.VMEM((HALVES, VOX, F, B), bf16),
            pltpu.VMEM((HALVES, VOX, F, B), bf16),
            pltpu.VMEM((SLOTS + 1, F, B), f32),
            pltpu.VMEM((SLOTS + 1, F, B), f32),
            pltpu.VMEM((SLOTS + 1, F, B), f32),
            pltpu.VMEM((VOX, F, B), f32),
            pltpu.VMEM((HALVES, OWN, F, B), bf16),
            pltpu.VMEM((HALVES, OWN, F, B), bf16),
            pltpu.VMEM((HALVES, OWN, F, B), bf16),
            pltpu.VMEM((HALVES, NY - 1, NZ, F, B), bf16),
            pltpu.VMEM((2, HALVES, NZ, F, B), bf16),
            pltpu.VMEM((2, HALVES, NZ - 1, NZ, F, B), bf16),
            pltpu.VMEM((RAYS, F, B), bf16),
            pltpu.VMEM((RAYS, F, B), bf16),
            pltpu.VMEM((NZ, ROUNDS, FP, B), bf16),
            dma((HALVES,)), dma((HALVES,)),
            dma((HALVES,)), dma((HALVES,)),
            dma((2, HALVES)), dma((2, HALVES)),
            dma((HALVES,)), dma((HALVES,)),
            dma((HALVES,)), dma((HALVES,)),
            dma((ROUNDS - 1, HALVES)), dma((ROUNDS - 1, HALVES)),
            dma((ROUNDS - 1, HALVES)), dma((ROUNDS - 1, HALVES)),
            dma, dma,
        ],
        compiler_params=pltpu.CompilerParams(collective_id=0, has_side_effects=True),
        name="fused",
    )(table, images, system_tiles, counts)


def solution(mesh):
    in_specs = (
        P("subset", "tile"),
        P("subset", "tile", None, None),
        P("subset", "tile"),
        P("subset", "tile"),
        P("subset", "tile"),
        P("subset", None, "tile"),
    )
    out_specs = P("subset", "tile")
    return jax.shard_map(shards, mesh=mesh, in_specs=in_specs, out_specs=out_specs, check_vma=False)
```

```python
import functools

import jax
import jax.numpy as jnp
from jax import lax
from jax.experimental import pallas as pl
from jax.experimental.pallas import tpu as pltpu
from jax.sharding import PartitionSpec as P

TILE_GROUP = 32
ROUNDS = 4
SUBSETS = 8
SLOTS = 32
VOX = 16
RAYS = 64
B = 128
NY = 8
NZ = 4
FP = 32
HALVES = 2
F = FP // HALVES
OWN = RAYS // 2
PARTS = 4

PREV_R, PREV_V, LAST_R, LAST_V, TABLE = 0, 1, 2, 3, 8

f32 = jnp.float32
bf16 = jnp.bfloat16


def fused(
    vox_of, ray_of, live, vox_row, ray_row, images_hbm, tiles_hbm, counts_hbm, out_hbm,
    images, tiles, counts, out, table_rows, table,
    low_0a, low_0b, low_1a, low_1b, low_2a, low_2b, low_3a, low_3b,
    rest, send_high, send_low, acc_a, acc_b, acc_back, inverse,
    send_c, recv_c, send_y, recv_y, send_z, recv_z, ratio_a, ratio_b, cnt,
    s_c, r_c, s_y, r_y, s_z, r_z, s_g, r_g, s_p, r_p, s_h, r_h, s_l, r_l, s_n, r_n,
    s_images, s_tiles, s_counts, s_table, s_out,
):
    low = ((low_0a, low_0b), (low_1a, low_1b), (low_2a, low_2b), (low_3a, low_3b))
    acc = (acc_a, acc_b)
    ratio = (ratio_a, ratio_b)
    subset = lax.axis_index("subset")
    tile = lax.axis_index("tile")
    core = lax.rem(tile, 2)
    z = lax.rem(lax.div(tile, 2), NZ)
    y = lax.div(tile, 2 * NZ)

    def at(y_of, z_of, c_of):
        return {"tile": (y_of * NZ + z_of) * 2 + c_of}

    partner = at(y, z, 1 - core)
    y_of = [None] + [lax.rem(y + k, NY) for k in range(1, NY)]
    y_peers = [None] + [at(y_of[k], z, core) for k in range(1, NY)]
    z_peers = [None] + [at(y, lax.rem(z + k, NZ), core) for k in range(1, NZ)]
    ahead = {"subset": lax.rem(subset + 1, SUBSETS)}
    behind = {"subset": lax.rem(subset + SUBSETS - 1, SUBSETS)}
    everyone = [partner] + y_peers[1:] + z_peers[1:] + [ahead, behind]
    far_first_y = (4, 3, 5, 2, 6, 1, 7)
    far_first_z = (2, 1, 3)

    barrier = pltpu.get_barrier_semaphore()
    for peer in everyone:
        pl.semaphore_signal(barrier, inc=1, device_id=peer, device_id_type=pl.DeviceIdType.MESH)

    def remote(src, dst, send, recv, peer):
        return pltpu.make_async_remote_copy(
            src_ref=src, dst_ref=dst, send_sem=send, recv_sem=recv,
            device_id=peer, device_id_type=pl.DeviceIdType.MESH,
        )

    def await_bytes(ref, sem):
        pltpu.make_async_copy(ref, ref, sem).wait()

    def frames(h):
        return slice(h * F, (h + 1) * F)

    copies = [pltpu.make_async_copy(images_hbm, images, s_images)]
    for i in range(PARTS):
        part = pl.ds(i * SLOTS // PARTS, SLOTS // PARTS)
        copies.append(pltpu.make_async_copy(tiles_hbm.at[0, part], tiles.at[part], s_tiles.at[i]))
    for r in range(ROUNDS):
        panel = lax.rem(subset - r + SUBSETS, SUBSETS)
        rows = pl.ds(pl.multiple_of(panel * FP, FP), FP)
        copies.append(pltpu.make_async_copy(counts_hbm.at[0, rows], counts.at[r], s_counts.at[r]))
    for copy in copies:
        copy.start()

    slot = lax.broadcasted_iota(jnp.int32, (SLOTS, SLOTS), 0)
    later = lax.broadcasted_iota(jnp.int32, (SLOTS, SLOTS), 1)

    def latest(found):
        best = jnp.max(jnp.where(found, lax.broadcasted_iota(jnp.int32, found.shape, 0), -1), axis=0, keepdims=True)
        return jnp.where(best < 0, SLOTS, best)

    for block_of, row, prev, last, blocks in (
        (ray_of, ray_row, PREV_R, LAST_R, RAYS),
        (vox_of, vox_row, PREV_V, LAST_V, VOX),
    ):
        column = jnp.zeros((SLOTS, B), jnp.int32)
        which = lax.broadcasted_iota(jnp.int32, (SLOTS, B), 0)
        for t in range(SLOTS):
            column = jnp.where(which == t, block_of[0, t], column)
        column = jnp.where(which // TILE_GROUP < live[0, 0], column, -1)
        same = column[:, :SLOTS] == jnp.broadcast_to(row[...], (SLOTS, SLOTS))
        table_rows[prev : prev + 1, :SLOTS] = latest(same & (slot < later))
        block = lax.broadcasted_iota(jnp.int32, (SLOTS, B), 1)
        table_rows[last : last + 1, :] = latest(column == block)
    table_copy = pltpu.make_async_copy(table_rows, table, s_table)
    table_copy.start()

    for h in range(HALVES):
        acc[h][SLOTS] = jnp.zeros((F, B), f32)
    acc_back[SLOTS] = jnp.zeros((F, B), f32)
    copies[0].wait()
    for h in range(HALVES):
        for v in range(VOX):
            low[0][h][v] = images[frames(h), v * B : (v + 1) * B].astype(bf16)
    table_copy.wait()

    def project(r, h):
        for t in range(SLOTS):
            if r == 0 and h == 0 and t % (SLOTS // PARTS) == 0:
                copies[1 + t // (SLOTS // PARTS)].wait()
            chosen = low[r][h][vox_of[0, t]]
            product = lax.dot_general(
                chosen, tiles[t], (((1,), (1,)), ((), ())), preferred_element_type=f32
            )
            acc[h][t] = product + acc[h][table[PREV_R, t]]
        for j in range(OWN):
            send_c[h, j] = acc[h][table[LAST_R, 2 * j + 1 - core]].astype(bf16)

    def backproject(h):
        for t in range(SLOTS):
            ray = ray_of[0, t]
            place = jnp.where(lax.rem(ray, 2) == core, 0, OWN) + lax.div(ray, 2)
            product = jnp.dot(ratio[h][place], tiles[t], preferred_element_type=f32)
            acc_back[t] = product + acc_back[table[PREV_V, t]]

    def stage_c(r, h):
        if r > 0:
            await_bytes(low[r][h], r_h.at[r - 1, h])
            await_bytes(send_c.at[h], s_c.at[h])
        project(r, h)
        if r == 0 and h == 0:
            pl.semaphore_wait(barrier, len(everyone))
        remote(send_c.at[h], recv_c.at[h], s_c.at[h], r_c.at[h], partner).start()

    def stage_y(r, h):
        await_bytes(recv_c.at[h], r_c.at[h])
        if r > 0:
            await_bytes(recv_y.at[h], s_y.at[h])
            await_bytes(ratio[h].at[pl.ds(0, OWN)], s_p.at[h])
        for j in range(OWN):
            own = acc[h][table[LAST_R, 2 * j + core]]
            send_y[h, j] = (own + recv_c[h, j].astype(f32)).astype(bf16)
        for k in far_first_y:
            remote(
                send_y.at[h, pl.ds(y_of[k] * NZ, NZ)], recv_y.at[h, k - 1],
                s_y.at[h], r_y.at[h], y_peers[k],
            ).start()

    def stage_z(r, h):
        p = r % 2
        await_bytes(recv_y.at[h], r_y.at[h])
        if r > 1:
            await_bytes(recv_z.at[p, h], s_z.at[p, h])
        for b in range(NZ):
            total = send_y[h, y * NZ + b].astype(f32)
            for k in range(NY - 1):
                total = total + recv_y[h, k, b].astype(f32)
            send_z[p, h, b] = total.astype(bf16)
        for k in far_first_z:
            remote(
                send_z.at[p, h], recv_z.at[p, h, k - 1], s_z.at[p, h], r_z.at[p, h], z_peers[k]
            ).start()

    def stage_g(r, h):
        p = r % 2
        await_bytes(recv_z.at[p, h], r_z.at[p, h])
        if r > 0:
            await_bytes(ratio[h].at[pl.ds(0, NZ * (NY - 1))], s_g.at[h])
        for b in range(NZ):
            even = send_z[p, h, b].astype(f32) + recv_z[p, h, 1, b].astype(f32)
            odd = recv_z[p, h, 0, b].astype(f32) + recv_z[p, h, 2, b].astype(f32)
            measured = cnt[b, r, frames(h), :].astype(f32)
            ratio[h][y * NZ + b] = (measured / (even + odd)).astype(bf16)
        mine = ratio[h].at[pl.ds(y * NZ, NZ)]
        for k in far_first_y:
            remote(mine, mine, s_g.at[h], r_g.at[h], y_peers[k]).start()

    def stage_p(h):
        await_bytes(ratio[h].at[pl.ds(0, NZ * (NY - 1))], r_g.at[h])
        remote(
            ratio[h].at[pl.ds(0, OWN)], ratio[h].at[pl.ds(OWN, OWN)], s_p.at[h], r_p.at[h], partner
        ).start()

    def stage_b(r, h):
        last = r + 1 == ROUNDS
        await_bytes(ratio[h].at[pl.ds(OWN, OWN)], r_p.at[h])
        backproject(h)
        if r > 0:
            await_bytes(rest.at[r - 1, h], r_l.at[r - 1, h])
            if not last:
                await_bytes(send_high.at[h], s_h.at[r - 1, h])
                await_bytes(send_low.at[h], s_l.at[r - 1, h])
        for v in range(VOX):
            if r == 0:
                held = images[frames(h), v * B : (v + 1) * B]
            else:
                held = low[r][h][v].astype(f32) + rest[r - 1, h, v].astype(f32)
            held = held * acc_back[table[LAST_V, v]] * inverse[v]
            if last:
                out[frames(h), v * B : (v + 1) * B] = held
            else:
                high = held.astype(bf16)
                send_high[h, v] = high
                send_low[h, v] = (held - high.astype(f32)).astype(bf16)
        if last:
            pltpu.make_async_copy(out.at[frames(h)], out_hbm.at[frames(h)], s_out.at[h]).start()
        else:
            remote(send_high.at[h], low[r + 1][h], s_h.at[r, h], r_h.at[r, h], ahead).start()
            remote(send_low.at[h], rest.at[r, h], s_l.at[r, h], r_l.at[r, h], ahead).start()

    def sensitivity():
        ones = jnp.ones((F, B), bf16)
        for t in range(SLOTS):
            column = jnp.dot(ones, tiles[t], preferred_element_type=f32)
            acc_back[t] = column + acc_back[table[PREV_V, t]]
        for v in range(VOX):
            inverse[v] = 1.0 / acc_back[table[LAST_V, v]]

    for r in range(ROUNDS):
        stage_c(r, 0)
        stage_y(r, 0)
        stage_c(r, 1)
        stage_y(r, 1)
        if r == 0:
            for i in range(ROUNDS):
                copies[1 + PARTS + i].wait()
                cnt[z, i] = counts[i].astype(f32).astype(bf16)
            for k in far_first_z:
                remote(cnt.at[z], cnt.at[z], s_n, r_n, z_peers[k]).start()
            sensitivity()
        stage_z(r, 0)
        stage_z(r, 1)
        if r == 0:
            await_bytes(cnt.at[pl.ds(0, NZ - 1)], r_n)
        stage_g(r, 0)
        stage_g(r, 1)
        stage_p(0)
        stage_b(r, 0)
        stage_p(1)
        stage_b(r, 1)

    await_bytes(cnt.at[pl.ds(0, NZ - 1)], s_n)
    for h in range(HALVES):
        await_bytes(send_c.at[h], s_c.at[h])
        await_bytes(recv_y.at[h], s_y.at[h])
        for p in range(2):
            await_bytes(recv_z.at[p, h], s_z.at[p, h])
        await_bytes(ratio[h].at[pl.ds(0, NZ * (NY - 1))], s_g.at[h])
        await_bytes(ratio[h].at[pl.ds(0, OWN)], s_p.at[h])
        await_bytes(send_high.at[h], s_h.at[ROUNDS - 2, h])
        await_bytes(send_low.at[h], s_l.at[ROUNDS - 2, h])
        pltpu.make_async_copy(out.at[frames(h)], out_hbm.at[frames(h)], s_out.at[h]).wait()


def shards(images, system_tiles, tile_vox, tile_ray, live_blocks, counts):
    smem = pl.BlockSpec(memory_space=pltpu.SMEM)
    vmem = pl.BlockSpec(memory_space=pltpu.VMEM)
    hbm = pl.BlockSpec(memory_space=pl.ANY)
    half = pltpu.VMEM((VOX, F, B), bf16)
    dma = pltpu.SemaphoreType.DMA
    return pl.pallas_call(
        fused,
        out_shape=jax.ShapeDtypeStruct(images.shape, f32),
        in_specs=[smem, smem, smem, vmem, vmem, hbm, hbm, hbm],
        out_specs=hbm,
        scratch_shapes=[
            pltpu.VMEM((FP, VOX * B), f32),
            pltpu.VMEM((SLOTS, B, B), bf16),
            pltpu.VMEM((ROUNDS, FP, B), jnp.int32),
            pltpu.VMEM((FP, VOX * B), f32),
            pltpu.VMEM((TABLE, B), jnp.int32),
            pltpu.SMEM((TABLE, B), jnp.int32),
        ]
        + [half] * (2 * ROUNDS)
        + [
            pltpu.VMEM((ROUNDS - 1, HALVES, VOX, F, B), bf16),
            pltpu.VMEM((HALVES, VOX, F, B), bf16),
            pltpu.VMEM((HALVES, VOX, F, B), bf16),
            pltpu.VMEM((SLOTS + 1, F, B), f32),
            pltpu.VMEM((SLOTS + 1, F, B), f32),
            pltpu.VMEM((SLOTS + 1, F, B), f32),
            pltpu.VMEM((VOX, F, B), f32),
            pltpu.VMEM((HALVES, OWN, F, B), bf16),
            pltpu.VMEM((HALVES, OWN, F, B), bf16),
            pltpu.VMEM((HALVES, OWN, F, B), bf16),
            pltpu.VMEM((HALVES, NY - 1, NZ, F, B), bf16),
            pltpu.VMEM((2, HALVES, NZ, F, B), bf16),
            pltpu.VMEM((2, HALVES, NZ - 1, NZ, F, B), bf16),
            pltpu.VMEM((RAYS, F, B), bf16),
            pltpu.VMEM((RAYS, F, B), bf16),
            pltpu.VMEM((NZ, ROUNDS, FP, B), bf16),
            dma((HALVES,)), dma((HALVES,)),
            dma((HALVES,)), dma((HALVES,)),
            dma((2, HALVES)), dma((2, HALVES)),
            dma((HALVES,)), dma((HALVES,)),
            dma((HALVES,)), dma((HALVES,)),
            dma((ROUNDS - 1, HALVES)), dma((ROUNDS - 1, HALVES)),
            dma((ROUNDS - 1, HALVES)), dma((ROUNDS - 1, HALVES)),
            dma, dma,
            dma, dma((PARTS,)), dma((ROUNDS,)), dma, dma((HALVES,)),
        ],
        compiler_params=pltpu.CompilerParams(collective_id=0, has_side_effects=True),
        name="fused",
    )(tile_vox, tile_ray, live_blocks, tile_vox, tile_ray, images, system_tiles, counts)


def solution(mesh):
    in_specs = (
        P("subset", "tile"),
        P("subset", "tile", None, None),
        P("subset", "tile"),
        P("subset", "tile"),
        P("subset", "tile"),
        P("subset", None, "tile"),
    )
    out_specs = P("subset", "tile")
    return jax.shard_map(shards, mesh=mesh, in_specs=in_specs, out_specs=out_specs, check_vma=False)
```

```python
import functools

import jax
import jax.numpy as jnp
from jax import lax
from jax.experimental import pallas as pl
from jax.experimental.pallas import tpu as pltpu
from jax.sharding import PartitionSpec as P

TILE_GROUP = 32
ROUNDS = 4
SUBSETS = 8
SLOTS = 32
VOX = 16
RAYS = 64
B = 128
NY = 8
NZ = 4
FP = 32
HALVES = 2
F = FP // HALVES
OWN = RAYS // 2
PARTS = 4
PIECES = 8
LENT = 2
OWN_ROUNDS = (0, 1, 3)

PREV_R, PREV_V, LAST_R, LAST_V, PLACE, VOX_OF, TABLE = 0, 1, 2, 3, 4, 5, 8

f32 = jnp.float32
bf16 = jnp.bfloat16


def fused(
    images_hbm, tiles_hbm, vox_hbm, ray_hbm, live_hbm, counts_hbm, out_hbm,
    vox_of, ray_of, live, vox_row, ray_row, images, own_tiles, counts, out, table_rows, own_table,
    lent_tiles, lent_rows, lent_table, lent_inverse, count_out, count_in, lent_cnt,
    low_0a, low_0b, low_1a, low_1b, low_2a, low_2b, low_3a, low_3b,
    rest, send_high, send_low, acc_a, acc_b, acc_back, own_inverse,
    send_c, recv_c, send_y, recv_y, send_z, recv_z, ratio_a, ratio_b, cnt,
    s_c, r_c, s_y, r_y, s_z, r_z, s_g, r_g, s_p, r_p, s_h, r_h, s_l, r_l, s_n, r_n,
    s_index, s_images, s_tiles, s_counts, s_table, s_out,
    s_t, r_t, s_i, r_i, s_k, r_k, s_m, r_m,
):
    low = ((low_0a, low_0b), (low_1a, low_1b), (low_2a, low_2b), (low_3a, low_3b))
    acc = (acc_a, acc_b)
    ratio = (ratio_a, ratio_b)
    subset = lax.axis_index("subset")
    tile = lax.axis_index("tile")
    core = lax.rem(tile, 2)
    z = lax.rem(lax.div(tile, 2), NZ)
    y = lax.div(tile, 2 * NZ)

    def at(y_of, z_of, c_of):
        return {"tile": (y_of * NZ + z_of) * 2 + c_of}

    partner = at(y, z, 1 - core)
    y_of = [None] + [lax.rem(y + k, NY) for k in range(1, NY)]
    y_peers = [None] + [at(y_of[k], z, core) for k in range(1, NY)]
    z_peers = [None] + [at(y, lax.rem(z + k, NZ), core) for k in range(1, NZ)]
    ahead = {"subset": lax.rem(subset + 1, SUBSETS)}
    behind = {"subset": lax.rem(subset + SUBSETS - 1, SUBSETS)}
    ahead_two = {"subset": lax.rem(subset + 2, SUBSETS)}
    behind_two = {"subset": lax.rem(subset + SUBSETS - 2, SUBSETS)}
    everyone = [partner] + y_peers[1:] + z_peers[1:] + [ahead, behind, ahead_two, behind_two]
    far_first_y = (4, 3, 5, 2, 6, 1, 7)
    far_first_z = (2, 1, 3)

    barrier = pltpu.get_barrier_semaphore()
    for peer in everyone:
        pl.semaphore_signal(barrier, inc=1, device_id=peer, device_id_type=pl.DeviceIdType.MESH)

    def remote(src, dst, send, recv, peer):
        return pltpu.make_async_remote_copy(
            src_ref=src, dst_ref=dst, send_sem=send, recv_sem=recv,
            device_id=peer, device_id_type=pl.DeviceIdType.MESH,
        )

    def await_bytes(ref, sem):
        pltpu.make_async_copy(ref, ref, sem).wait()

    def frames(h):
        return slice(h * F, (h + 1) * F)

    indices = [
        pltpu.make_async_copy(src, dst, s_index.at[i])
        for i, (src, dst) in enumerate(
            ((vox_hbm, vox_of), (ray_hbm, ray_of), (live_hbm, live), (vox_hbm, vox_row), (ray_hbm, ray_row))
        )
    ]
    for copy in indices:
        copy.start()
    copies = [pltpu.make_async_copy(images_hbm, images, s_images)]
    for i in range(PARTS):
        part = pl.ds(i * SLOTS // PARTS, SLOTS // PARTS)
        copies.append(pltpu.make_async_copy(tiles_hbm.at[0, part], own_tiles.at[part], s_tiles.at[i]))
    for r in range(ROUNDS):
        panel = lax.rem(subset - r + SUBSETS, SUBSETS)
        rows = pl.ds(pl.multiple_of(panel * FP, FP), FP)
        copies.append(pltpu.make_async_copy(counts_hbm.at[0, rows], counts.at[r], s_counts.at[r]))
    for copy in copies:
        copy.start()
    for copy in indices:
        copy.wait()

    slot = lax.broadcasted_iota(jnp.int32, (SLOTS, SLOTS), 0)
    later = lax.broadcasted_iota(jnp.int32, (SLOTS, SLOTS), 1)

    def latest(found):
        best = jnp.max(jnp.where(found, lax.broadcasted_iota(jnp.int32, found.shape, 0), -1), axis=0, keepdims=True)
        return jnp.where(best < 0, SLOTS, best)

    for block_of, row, prev, last, blocks in (
        (ray_of, ray_row, PREV_R, LAST_R, RAYS),
        (vox_of, vox_row, PREV_V, LAST_V, VOX),
    ):
        column = jnp.zeros((SLOTS, B), jnp.int32)
        which = lax.broadcasted_iota(jnp.int32, (SLOTS, B), 0)
        for t in range(SLOTS):
            column = jnp.where(which == t, block_of[0, t], column)
        column = jnp.where(which // TILE_GROUP < live[0, 0], column, -1)
        same = column[:, :SLOTS] == jnp.broadcast_to(row[...], (SLOTS, SLOTS))
        table_rows[prev : prev + 1, :SLOTS] = latest(same & (slot < later))
        block = lax.broadcasted_iota(jnp.int32, (SLOTS, B), 1)
        table_rows[last : last + 1, :] = latest(column == block)
    ray = ray_row[...]
    place = jnp.where(ray % 2 == core, 0, OWN) + ray // 2
    table_rows[PLACE : PLACE + 1, :SLOTS] = place
    table_rows[VOX_OF : VOX_OF + 1, :SLOTS] = vox_row[...]
    table_copy = pltpu.make_async_copy(table_rows, own_table, s_table.at[0])
    table_copy.start()

    for h in range(HALVES):
        acc[h][SLOTS] = jnp.zeros((F, B), f32)
    acc_back[SLOTS] = jnp.zeros((F, B), f32)
    copies[0].wait()
    for h in range(HALVES):
        for v in range(VOX):
            low[0][h][v] = images[frames(h), v * B : (v + 1) * B].astype(bf16)
    table_copy.wait()

    def with_tiles(r):
        return (lent_tiles, lent_table, lent_inverse) if r == LENT else (own_tiles, own_table, own_inverse)

    def project(r, h):
        tiles, table, _ = with_tiles(r)
        for t in range(0, SLOTS, 2):
            if r == 0 and h == 0 and t % (SLOTS // PARTS) == 0:
                copies[1 + t // (SLOTS // PARTS)].wait()
            chosen = jnp.concatenate([low[r][h][table[VOX_OF, t + i]] for i in range(2)], axis=0)
            pair = tiles[t : t + 2].reshape(2 * B, B)
            product = lax.dot_general(
                chosen, pair, (((1,), (1,)), ((), ())), preferred_element_type=f32
            )
            for i in range(2):
                mine = product[i * F : (i + 1) * F, i * B : (i + 1) * B]
                acc[h][t + i] = mine + acc[h][table[PREV_R, t + i]]
        for j in range(OWN):
            send_c[h, j] = acc[h][table[LAST_R, 2 * j + 1 - core]].astype(bf16)

    def backproject(r, h):
        tiles, table, _ = with_tiles(r)
        for t in range(0, SLOTS, 2):
            chosen = jnp.concatenate([ratio[h][table[PLACE, t + i]] for i in range(2)], axis=0)
            pair = jnp.concatenate([tiles[t], tiles[t + 1]], axis=1)
            product = jnp.dot(chosen, pair, preferred_element_type=f32)
            for i in range(2):
                mine = product[i * F : (i + 1) * F, i * B : (i + 1) * B]
                acc_back[t + i] = mine + acc_back[table[PREV_V, t + i]]

    def stage_c(r, h):
        if 0 < r <= LENT:
            await_bytes(low[r][h], r_h.at[r - 1, h])
        if r > 0:
            await_bytes(send_c.at[h], s_c.at[h])
        project(r, h)
        if r == 0 and h == 0:
            pl.semaphore_wait(barrier, len(everyone))
        remote(send_c.at[h], recv_c.at[h], s_c.at[h], r_c.at[h], partner).start()

    def stage_y(r, h):
        table = with_tiles(r)[1]
        await_bytes(recv_c.at[h], r_c.at[h])
        if r > 0:
            await_bytes(recv_y.at[h], s_y.at[h])
            await_bytes(ratio[h].at[pl.ds(0, OWN)], s_p.at[h])
        for j in range(OWN):
            own = acc[h][table[LAST_R, 2 * j + core]]
            send_y[h, j] = (own + recv_c[h, j].astype(f32)).astype(bf16)
        for k in far_first_y:
            remote(
                send_y.at[h, pl.ds(y_of[k] * NZ, NZ)], recv_y.at[h, k - 1],
                s_y.at[h], r_y.at[h], y_peers[k],
            ).start()

    def stage_z(r, h):
        p = r % 2
        await_bytes(recv_y.at[h], r_y.at[h])
        if r > 1:
            await_bytes(recv_z.at[p, h], s_z.at[p, h])
        for b in range(NZ):
            total = send_y[h, y * NZ + b].astype(f32)
            for k in range(NY - 1):
                total = total + recv_y[h, k, b].astype(f32)
            send_z[p, h, b] = total.astype(bf16)
        for k in far_first_z:
            remote(
                send_z.at[p, h], recv_z.at[p, h, k - 1], s_z.at[p, h], r_z.at[p, h], z_peers[k]
            ).start()

    def stage_g(r, h):
        p = r % 2
        await_bytes(recv_z.at[p, h], r_z.at[p, h])
        if r > 0:
            await_bytes(ratio[h].at[pl.ds(0, NZ * (NY - 1))], s_g.at[h])
        for b in range(NZ):
            even = send_z[p, h, b].astype(f32) + recv_z[p, h, 1, b].astype(f32)
            odd = recv_z[p, h, 0, b].astype(f32) + recv_z[p, h, 2, b].astype(f32)
            if r == LENT:
                measured = lent_cnt[b, frames(h), :].astype(f32)
            else:
                measured = cnt[b, OWN_ROUNDS.index(r), frames(h), :].astype(f32)
            ratio[h][y * NZ + b] = (measured / (even + odd)).astype(bf16)
        mine = ratio[h].at[pl.ds(y * NZ, NZ)]
        for k in far_first_y:
            remote(mine, mine, s_g.at[h], r_g.at[h], y_peers[k]).start()

    def stage_p(h):
        await_bytes(ratio[h].at[pl.ds(0, NZ * (NY - 1))], r_g.at[h])
        remote(
            ratio[h].at[pl.ds(0, OWN)], ratio[h].at[pl.ds(OWN, OWN)], s_p.at[h], r_p.at[h], partner
        ).start()

    def stage_b(r, h):
        last = r + 1 == ROUNDS
        _, table, inverse = with_tiles(r)
        await_bytes(ratio[h].at[pl.ds(OWN, OWN)], r_p.at[h])
        backproject(r, h)
        if 0 < r <= LENT:
            await_bytes(rest.at[r - 1, h], r_l.at[r - 1, h])
        if r == 1:
            await_bytes(send_high.at[h], s_h.at[r - 1, h])
            await_bytes(send_low.at[h], s_l.at[r - 1, h])
        for v in range(VOX):
            if r == 0:
                held = images[frames(h), v * B : (v + 1) * B]
            elif r <= LENT:
                held = low[r][h][v].astype(f32) + rest[r - 1, h, v].astype(f32)
            else:
                held = out[frames(h), v * B : (v + 1) * B]
            held = held * acc_back[table[LAST_V, v]] * inverse[v]
            if r >= LENT:
                out[frames(h), v * B : (v + 1) * B] = held
                if not last:
                    low[r + 1][h][v] = held.astype(bf16)
            else:
                high = held.astype(bf16)
                send_high[h, v] = high
                send_low[h, v] = (held - high.astype(f32)).astype(bf16)
        if last:
            pltpu.make_async_copy(out.at[frames(h)], out_hbm.at[frames(h)], s_out.at[h]).start()
        elif r < LENT:
            target = ahead if r == 0 else ahead_two
            remote(send_high.at[h], low[r + 1][h], s_h.at[r, h], r_h.at[r, h], target).start()
            remote(send_low.at[h], rest.at[r, h], s_l.at[r, h], r_l.at[r, h], target).start()

    def sensitivity(r):
        tiles, table, inverse = with_tiles(r)
        ones = jnp.ones((F, B), bf16)
        for t in range(SLOTS):
            column = jnp.dot(ones, tiles[t], preferred_element_type=f32)
            acc_back[t] = column + acc_back[table[PREV_V, t]]
        for v in range(VOX):
            inverse[v] = 1.0 / acc_back[table[LAST_V, v]]

    def lend(i):
        part = pl.ds(i * SLOTS // PIECES, SLOTS // PIECES)
        remote(own_tiles.at[part], lent_tiles.at[part], s_t, r_t, ahead).start()

    def share_counts():
        for k in far_first_z:
            remote(cnt.at[z], cnt.at[z], s_n, r_n, z_peers[k]).start()
        remote(count_out, count_in, s_k, r_k, ahead).start()
        remote(table_rows, lent_rows, s_i, r_i, ahead).start()

    def take_lent():
        await_bytes(count_in, r_k)
        lent_cnt[z] = count_in[...]
        for k in far_first_z:
            remote(lent_cnt.at[z], lent_cnt.at[z], s_m, r_m, z_peers[k]).start()
        await_bytes(lent_rows, r_i)
        lent_copy = pltpu.make_async_copy(lent_rows, lent_table, s_table.at[1])
        lent_copy.start()
        lent_copy.wait()

    for i in range(ROUNDS):
        copies[1 + PARTS + i].wait()
        measured = counts[i].astype(f32).astype(bf16)
        if i == LENT:
            count_out[...] = measured
        else:
            cnt[z, OWN_ROUNDS.index(i)] = measured

    for r in range(ROUNDS):
        stage_c(r, 0)
        if r == 0:
            share_counts()
        if r == LENT + 1:
            stage_p(1)
        stage_y(r, 0)
        if r == LENT + 1:
            stage_b(LENT, 1)
        if r < LENT:
            lend(4 * r)
        stage_c(r, 1)
        stage_y(r, 1)
        if r < LENT:
            lend(4 * r + 1)
        if r in (0, LENT):
            sensitivity(r)
        stage_z(r, 0)
        stage_z(r, 1)
        if r == 0:
            await_bytes(cnt.at[pl.ds(0, NZ - 1)], r_n)
        if r == LENT:
            await_bytes(lent_cnt.at[pl.ds(0, NZ - 1)], r_m)
        stage_g(r, 0)
        stage_g(r, 1)
        if r < LENT:
            lend(4 * r + 2)
            lend(4 * r + 3)
        if r + 1 == LENT:
            take_lent()
        stage_p(0)
        stage_b(r, 0)
        if r != LENT:
            stage_p(1)
            stage_b(r, 1)
        if r + 1 == LENT:
            await_bytes(lent_tiles, r_t)

    await_bytes(own_tiles, s_t)
    await_bytes(table_rows, s_i)
    await_bytes(count_out, s_k)
    await_bytes(lent_cnt.at[pl.ds(0, NZ - 1)], s_m)
    await_bytes(cnt.at[pl.ds(0, NZ - 1)], s_n)
    for h in range(HALVES):
        await_bytes(send_c.at[h], s_c.at[h])
        await_bytes(recv_y.at[h], s_y.at[h])
        for p in range(2):
            await_bytes(recv_z.at[p, h], s_z.at[p, h])
        await_bytes(ratio[h].at[pl.ds(0, NZ * (NY - 1))], s_g.at[h])
        await_bytes(ratio[h].at[pl.ds(0, OWN)], s_p.at[h])
        await_bytes(send_high.at[h], s_h.at[LENT - 1, h])
        await_bytes(send_low.at[h], s_l.at[LENT - 1, h])
        pltpu.make_async_copy(out.at[frames(h)], out_hbm.at[frames(h)], s_out.at[h]).wait()


def shards(images, system_tiles, tile_vox, tile_ray, live_blocks, counts):
    hbm = pl.BlockSpec(memory_space=pl.ANY)
    half = pltpu.VMEM((VOX, F, B), bf16)
    dma = pltpu.SemaphoreType.DMA
    return pl.pallas_call(
        fused,
        out_shape=jax.ShapeDtypeStruct(images.shape, f32),
        in_specs=[hbm] * 6,
        out_specs=hbm,
        scratch_shapes=[
            pltpu.SMEM((1, SLOTS), jnp.int32),
            pltpu.SMEM((1, SLOTS), jnp.int32),
            pltpu.SMEM((1, 1), jnp.int32),
            pltpu.VMEM((1, SLOTS), jnp.int32),
            pltpu.VMEM((1, SLOTS), jnp.int32),
            pltpu.VMEM((FP, VOX * B), f32),
            pltpu.VMEM((SLOTS, B, B), bf16),
            pltpu.VMEM((ROUNDS, FP, B), jnp.int32),
            pltpu.VMEM((FP, VOX * B), f32),
            pltpu.VMEM((TABLE, B), jnp.int32),
            pltpu.SMEM((TABLE, B), jnp.int32),
            pltpu.VMEM((SLOTS, B, B), bf16),
            pltpu.VMEM((TABLE, B), jnp.int32),
            pltpu.SMEM((TABLE, B), jnp.int32),
            pltpu.VMEM((VOX, F, B), f32),
            pltpu.VMEM((FP, B), bf16),
            pltpu.VMEM((FP, B), bf16),
            pltpu.VMEM((NZ, FP, B), bf16),
        ]
        + [half] * (2 * ROUNDS)
        + [
            pltpu.VMEM((LENT, HALVES, VOX, F, B), bf16),
            pltpu.VMEM((HALVES, VOX, F, B), bf16),
            pltpu.VMEM((HALVES, VOX, F, B), bf16),
            pltpu.VMEM((SLOTS + 1, F, B), f32),
            pltpu.VMEM((SLOTS + 1, F, B), f32),
            pltpu.VMEM((SLOTS + 1, F, B), f32),
            pltpu.VMEM((VOX, F, B), f32),
            pltpu.VMEM((HALVES, OWN, F, B), bf16),
            pltpu.VMEM((HALVES, OWN, F, B), bf16),
            pltpu.VMEM((HALVES, OWN, F, B), bf16),
            pltpu.VMEM((HALVES, NY - 1, NZ, F, B), bf16),
            pltpu.VMEM((2, HALVES, NZ, F, B), bf16),
            pltpu.VMEM((2, HALVES, NZ - 1, NZ, F, B), bf16),
            pltpu.VMEM((RAYS, F, B), bf16),
            pltpu.VMEM((RAYS, F, B), bf16),
            pltpu.VMEM((NZ, len(OWN_ROUNDS), FP, B), bf16),
            dma((HALVES,)), dma((HALVES,)),
            dma((HALVES,)), dma((HALVES,)),
            dma((2, HALVES)), dma((2, HALVES)),
            dma((HALVES,)), dma((HALVES,)),
            dma((HALVES,)), dma((HALVES,)),
            dma((LENT, HALVES)), dma((LENT, HALVES)),
            dma((LENT, HALVES)), dma((LENT, HALVES)),
            dma, dma,
            dma((5,)), dma, dma((PARTS,)), dma((ROUNDS,)), dma((2,)), dma((HALVES,)),
            dma, dma, dma, dma, dma, dma, dma, dma,
        ],
        compiler_params=pltpu.CompilerParams(collective_id=0, has_side_effects=True),
        name="fused",
    )(images, system_tiles, tile_vox, tile_ray, live_blocks, counts)


def solution(mesh):
    in_specs = (
        P("subset", "tile"),
        P("subset", "tile", None, None),
        P("subset", "tile"),
        P("subset", "tile"),
        P("subset", "tile"),
        P("subset", None, "tile"),
    )
    out_specs = P("subset", "tile")
    return jax.shard_map(shards, mesh=mesh, in_specs=in_specs, out_specs=out_specs, check_vma=False)
```

```python
import functools

import jax
import jax.numpy as jnp
from jax import lax
from jax.experimental import pallas as pl
from jax.experimental.pallas import tpu as pltpu
from jax.sharding import PartitionSpec as P

TILE_GROUP = 32
ROUNDS = 4
SUBSETS = 8
SLOTS = 32
VOX = 16
RAYS = 64
B = 128
NY = 8
NZ = 4
FP = 32
HALVES = 2
F = FP // HALVES
OWN = RAYS // 2
PARTS = 4
PIECES = 8
LENT = 2
OWN_ROUNDS = (0, 1, 3)

PREV_R, PREV_V, LAST_R, LAST_V, PLACE, VOX_OF, TABLE = 0, 1, 2, 3, 4, 5, 8

f32 = jnp.float32
bf16 = jnp.bfloat16


def fused(
    images_hbm, tiles_hbm, vox_hbm, ray_hbm, live_hbm, counts_hbm, out,
    vox_of, ray_of, live, vox_row, ray_row, images, own_tiles, counts, table_rows, own_table,
    lent_tiles, lent_rows, lent_table, lent_inverse, count_out, count_in, lent_cnt,
    low_0a, low_0b, low_1a, low_1b, low_2a, low_2b, low_3a, low_3b,
    rest, send_high, send_low, acc_a, acc_b, acc_back, own_inverse,
    send_c, recv_c, send_y, recv_y, send_z, recv_z, ratio_a, ratio_b, cnt,
    s_c, r_c, s_y, r_y, s_z, r_z, s_g, r_g, s_p, r_p, s_h, r_h, s_l, r_l, s_n, r_n,
    s_index, s_images, s_tiles, s_counts, s_table,
    s_t, r_t, s_i, r_i, s_k, r_k, s_m, r_m,
):
    low = ((low_0a, low_0b), (low_1a, low_1b), (low_2a, low_2b), (low_3a, low_3b))
    acc = (acc_a, acc_b)
    ratio = (ratio_a, ratio_b)
    subset = lax.axis_index("subset")
    tile = lax.axis_index("tile")
    core = lax.rem(tile, 2)
    z = lax.rem(lax.div(tile, 2), NZ)
    y = lax.div(tile, 2 * NZ)

    def at(y_of, z_of, c_of):
        return {"tile": (y_of * NZ + z_of) * 2 + c_of}

    partner = at(y, z, 1 - core)
    y_of = [None] + [lax.rem(y + k, NY) for k in range(1, NY)]
    y_peers = [None] + [at(y_of[k], z, core) for k in range(1, NY)]
    z_peers = [None] + [at(y, lax.rem(z + k, NZ), core) for k in range(1, NZ)]
    ahead = {"subset": lax.rem(subset + 1, SUBSETS)}
    behind = {"subset": lax.rem(subset + SUBSETS - 1, SUBSETS)}
    ahead_two = {"subset": lax.rem(subset + 2, SUBSETS)}
    behind_two = {"subset": lax.rem(subset + SUBSETS - 2, SUBSETS)}
    everyone = [partner] + y_peers[1:] + z_peers[1:] + [ahead, behind, ahead_two, behind_two]
    far_first_y = (4, 3, 5, 2, 6, 1, 7)
    far_first_z = (2, 1, 3)

    barrier = pltpu.get_barrier_semaphore()
    for peer in everyone:
        pl.semaphore_signal(barrier, inc=1, device_id=peer, device_id_type=pl.DeviceIdType.MESH)

    def remote(src, dst, send, recv, peer):
        return pltpu.make_async_remote_copy(
            src_ref=src, dst_ref=dst, send_sem=send, recv_sem=recv,
            device_id=peer, device_id_type=pl.DeviceIdType.MESH,
        )

    def await_bytes(ref, sem):
        pltpu.make_async_copy(ref, ref, sem).wait()

    def frames(h):
        return slice(h * F, (h + 1) * F)

    indices = [
        pltpu.make_async_copy(src, dst, s_index.at[i])
        for i, (src, dst) in enumerate(
            ((vox_hbm, vox_of), (ray_hbm, ray_of), (live_hbm, live), (vox_hbm, vox_row), (ray_hbm, ray_row))
        )
    ]
    for copy in indices:
        copy.start()
    copies = [pltpu.make_async_copy(images_hbm, images, s_images)]
    for i in range(PARTS):
        part = pl.ds(i * SLOTS // PARTS, SLOTS // PARTS)
        copies.append(pltpu.make_async_copy(tiles_hbm.at[0, part], own_tiles.at[part], s_tiles.at[i]))
    for r in range(ROUNDS):
        panel = lax.rem(subset - r + SUBSETS, SUBSETS)
        rows = pl.ds(pl.multiple_of(panel * FP, FP), FP)
        copies.append(pltpu.make_async_copy(counts_hbm.at[0, rows], counts.at[r], s_counts.at[r]))
    for copy in copies:
        copy.start()
    for copy in indices:
        copy.wait()

    slot = lax.broadcasted_iota(jnp.int32, (SLOTS, SLOTS), 0)
    later = lax.broadcasted_iota(jnp.int32, (SLOTS, SLOTS), 1)

    def latest(found):
        best = jnp.max(jnp.where(found, lax.broadcasted_iota(jnp.int32, found.shape, 0), -1), axis=0, keepdims=True)
        return jnp.where(best < 0, SLOTS, best)

    for block_of, row, prev, last, blocks in (
        (ray_of, ray_row, PREV_R, LAST_R, RAYS),
        (vox_of, vox_row, PREV_V, LAST_V, VOX),
    ):
        column = jnp.zeros((SLOTS, B), jnp.int32)
        which = lax.broadcasted_iota(jnp.int32, (SLOTS, B), 0)
        for t in range(SLOTS):
            column = jnp.where(which == t, block_of[0, t], column)
        column = jnp.where(which // TILE_GROUP < live[0, 0], column, -1)
        same = column[:, :SLOTS] == jnp.broadcast_to(row[...], (SLOTS, SLOTS))
        table_rows[prev : prev + 1, :SLOTS] = latest(same & (slot < later))
        block = lax.broadcasted_iota(jnp.int32, (SLOTS, B), 1)
        table_rows[last : last + 1, :] = latest(column == block)
    ray = ray_row[...]
    place = jnp.where(ray % 2 == core, 0, OWN) + ray // 2
    table_rows[PLACE : PLACE + 1, :SLOTS] = place
    table_rows[VOX_OF : VOX_OF + 1, :SLOTS] = vox_row[...]
    table_copy = pltpu.make_async_copy(table_rows, own_table, s_table.at[0])
    table_copy.start()

    for h in range(HALVES):
        acc[h][SLOTS] = jnp.zeros((F, B), f32)
    acc_back[SLOTS] = jnp.zeros((F, B), f32)
    copies[0].wait()
    for h in range(HALVES):
        for v in range(VOX):
            low[0][h][v] = images[frames(h), v * B : (v + 1) * B].astype(bf16)
    table_copy.wait()

    def with_tiles(r):
        return (lent_tiles, lent_table, lent_inverse) if r == LENT else (own_tiles, own_table, own_inverse)

    def project(r, h):
        tiles, table, _ = with_tiles(r)
        for t in range(0, SLOTS, 2):
            if r == 0 and h == 0 and t % (SLOTS // PARTS) == 0:
                copies[1 + t // (SLOTS // PARTS)].wait()
            chosen = jnp.concatenate([low[r][h][table[VOX_OF, t + i]] for i in range(2)], axis=0)
            pair = tiles[t : t + 2].reshape(2 * B, B)
            product = lax.dot_general(
                chosen, pair, (((1,), (1,)), ((), ())), preferred_element_type=f32
            )
            for i in range(2):
                mine = product[i * F : (i + 1) * F, i * B : (i + 1) * B]
                acc[h][t + i] = mine + acc[h][table[PREV_R, t + i]]
        for j in range(OWN):
            send_c[h, j] = acc[h][table[LAST_R, 2 * j + 1 - core]].astype(bf16)

    def backproject(r, h):
        tiles, table, _ = with_tiles(r)
        for t in range(0, SLOTS, 2):
            chosen = jnp.concatenate([ratio[h][table[PLACE, t + i]] for i in range(2)], axis=0)
            pair = jnp.concatenate([tiles[t], tiles[t + 1]], axis=1)
            product = jnp.dot(chosen, pair, preferred_element_type=f32)
            for i in range(2):
                mine = product[i * F : (i + 1) * F, i * B : (i + 1) * B]
                acc_back[t + i] = mine + acc_back[table[PREV_V, t + i]]

    def stage_c(r, h):
        if 0 < r <= LENT:
            await_bytes(low[r][h], r_h.at[r - 1, h])
        if r > 0:
            await_bytes(send_c.at[h], s_c.at[h])
        project(r, h)
        if r == 0 and h == 0:
            pl.semaphore_wait(barrier, len(everyone))
        remote(send_c.at[h], recv_c.at[h], s_c.at[h], r_c.at[h], partner).start()

    def stage_y(r, h):
        table = with_tiles(r)[1]
        await_bytes(recv_c.at[h], r_c.at[h])
        if r > 0:
            await_bytes(recv_y.at[h], s_y.at[h])
            await_bytes(ratio[h].at[pl.ds(0, OWN)], s_p.at[h])
        for j in range(OWN):
            own = acc[h][table[LAST_R, 2 * j + core]]
            send_y[h, j] = (own + recv_c[h, j].astype(f32)).astype(bf16)
        for k in far_first_y:
            remote(
                send_y.at[h, pl.ds(y_of[k] * NZ, NZ)], recv_y.at[h, k - 1],
                s_y.at[h], r_y.at[h], y_peers[k],
            ).start()

    def stage_z(r, h):
        p = r % 2
        await_bytes(recv_y.at[h], r_y.at[h])
        if r > 1:
            await_bytes(recv_z.at[p, h], s_z.at[p, h])
        for b in range(NZ):
            total = send_y[h, y * NZ + b].astype(f32)
            for k in range(NY - 1):
                total = total + recv_y[h, k, b].astype(f32)
            send_z[p, h, b] = total.astype(bf16)
        for k in far_first_z:
            remote(
                send_z.at[p, h], recv_z.at[p, h, k - 1], s_z.at[p, h], r_z.at[p, h], z_peers[k]
            ).start()

    def stage_g(r, h):
        p = r % 2
        await_bytes(recv_z.at[p, h], r_z.at[p, h])
        if r > 0:
            await_bytes(ratio[h].at[pl.ds(0, NZ * (NY - 1))], s_g.at[h])
        for b in range(NZ):
            even = send_z[p, h, b].astype(f32) + recv_z[p, h, 1, b].astype(f32)
            odd = recv_z[p, h, 0, b].astype(f32) + recv_z[p, h, 2, b].astype(f32)
            if r == LENT:
                measured = lent_cnt[b, frames(h), :].astype(f32)
            else:
                measured = cnt[b, OWN_ROUNDS.index(r), frames(h), :].astype(f32)
            ratio[h][y * NZ + b] = (measured / (even + odd)).astype(bf16)
        mine = ratio[h].at[pl.ds(y * NZ, NZ)]
        for k in far_first_y:
            remote(mine, mine, s_g.at[h], r_g.at[h], y_peers[k]).start()

    def stage_p(h):
        await_bytes(ratio[h].at[pl.ds(0, NZ * (NY - 1))], r_g.at[h])
        remote(
            ratio[h].at[pl.ds(0, OWN)], ratio[h].at[pl.ds(OWN, OWN)], s_p.at[h], r_p.at[h], partner
        ).start()

    def stage_b(r, h):
        last = r + 1 == ROUNDS
        _, table, inverse = with_tiles(r)
        await_bytes(ratio[h].at[pl.ds(OWN, OWN)], r_p.at[h])
        backproject(r, h)
        if 0 < r <= LENT:
            await_bytes(rest.at[r - 1, h], r_l.at[r - 1, h])
        if r == 1:
            await_bytes(send_high.at[h], s_h.at[r - 1, h])
            await_bytes(send_low.at[h], s_l.at[r - 1, h])
        for v in range(VOX):
            if r == 0:
                held = images[frames(h), v * B : (v + 1) * B]
            elif r <= LENT:
                held = low[r][h][v].astype(f32) + rest[r - 1, h, v].astype(f32)
            else:
                held = out[frames(h), v * B : (v + 1) * B]
            held = held * acc_back[table[LAST_V, v]] * inverse[v]
            if r >= LENT:
                out[frames(h), v * B : (v + 1) * B] = held
                if not last:
                    low[r + 1][h][v] = held.astype(bf16)
            else:
                high = held.astype(bf16)
                send_high[h, v] = high
                send_low[h, v] = (held - high.astype(f32)).astype(bf16)
        if r < LENT:
            target = ahead if r == 0 else ahead_two
            remote(send_high.at[h], low[r + 1][h], s_h.at[r, h], r_h.at[r, h], target).start()
            remote(send_low.at[h], rest.at[r, h], s_l.at[r, h], r_l.at[r, h], target).start()

    def sensitivity(r):
        tiles, table, inverse = with_tiles(r)
        ones = jnp.ones((F, B), bf16)
        for t in range(SLOTS):
            column = jnp.dot(ones, tiles[t], preferred_element_type=f32)
            acc_back[t] = column + acc_back[table[PREV_V, t]]
        for v in range(VOX):
            inverse[v] = 1.0 / acc_back[table[LAST_V, v]]

    def lend(i):
        part = pl.ds(i * SLOTS // PIECES, SLOTS // PIECES)
        remote(own_tiles.at[part], lent_tiles.at[part], s_t, r_t, ahead).start()

    def share_counts():
        for k in far_first_z:
            remote(cnt.at[z], cnt.at[z], s_n, r_n, z_peers[k]).start()
        remote(count_out, count_in, s_k, r_k, ahead).start()
        remote(table_rows, lent_rows, s_i, r_i, ahead).start()

    def take_lent():
        await_bytes(count_in, r_k)
        lent_cnt[z] = count_in[...]
        for k in far_first_z:
            remote(lent_cnt.at[z], lent_cnt.at[z], s_m, r_m, z_peers[k]).start()
        await_bytes(lent_rows, r_i)
        lent_copy = pltpu.make_async_copy(lent_rows, lent_table, s_table.at[1])
        lent_copy.start()
        lent_copy.wait()

    for i in range(ROUNDS):
        copies[1 + PARTS + i].wait()
        measured = counts[i].astype(f32).astype(bf16)
        if i == LENT:
            count_out[...] = measured
        else:
            cnt[z, OWN_ROUNDS.index(i)] = measured

    for r in range(ROUNDS):
        stage_c(r, 0)
        if r == 0:
            share_counts()
        if r == LENT + 1:
            stage_p(1)
        stage_y(r, 0)
        if r == LENT + 1:
            stage_b(LENT, 1)
        if r < LENT:
            lend(4 * r)
        stage_c(r, 1)
        stage_y(r, 1)
        if r < LENT:
            lend(4 * r + 1)
        if r in (0, LENT):
            sensitivity(r)
        stage_z(r, 0)
        stage_z(r, 1)
        if r == 0:
            await_bytes(cnt.at[pl.ds(0, NZ - 1)], r_n)
        if r == LENT:
            await_bytes(lent_cnt.at[pl.ds(0, NZ - 1)], r_m)
        stage_g(r, 0)
        stage_g(r, 1)
        if r < LENT:
            lend(4 * r + 2)
            lend(4 * r + 3)
        if r + 1 == LENT:
            take_lent()
        stage_p(0)
        stage_b(r, 0)
        if r != LENT:
            stage_p(1)
            stage_b(r, 1)
        if r + 1 == LENT:
            await_bytes(lent_tiles, r_t)

    await_bytes(own_tiles, s_t)
    await_bytes(table_rows, s_i)
    await_bytes(count_out, s_k)
    await_bytes(lent_cnt.at[pl.ds(0, NZ - 1)], s_m)
    await_bytes(cnt.at[pl.ds(0, NZ - 1)], s_n)
    for h in range(HALVES):
        await_bytes(send_c.at[h], s_c.at[h])
        await_bytes(recv_y.at[h], s_y.at[h])
        for p in range(2):
            await_bytes(recv_z.at[p, h], s_z.at[p, h])
        await_bytes(ratio[h].at[pl.ds(0, NZ * (NY - 1))], s_g.at[h])
        await_bytes(ratio[h].at[pl.ds(0, OWN)], s_p.at[h])
        await_bytes(send_high.at[h], s_h.at[LENT - 1, h])
        await_bytes(send_low.at[h], s_l.at[LENT - 1, h])


def shards(images, system_tiles, tile_vox, tile_ray, live_blocks, counts):
    hbm = pl.BlockSpec(memory_space=pl.ANY)
    half = pltpu.VMEM((VOX, F, B), bf16)
    dma = pltpu.SemaphoreType.DMA
    return pl.pallas_call(
        fused,
        out_shape=jax.ShapeDtypeStruct(images.shape, f32),
        in_specs=[hbm] * 6,
        out_specs=pl.BlockSpec(memory_space=pltpu.VMEM),
        scratch_shapes=[
            pltpu.SMEM((1, SLOTS), jnp.int32),
            pltpu.SMEM((1, SLOTS), jnp.int32),
            pltpu.SMEM((1, 1), jnp.int32),
            pltpu.VMEM((1, SLOTS), jnp.int32),
            pltpu.VMEM((1, SLOTS), jnp.int32),
            pltpu.VMEM((FP, VOX * B), f32),
            pltpu.VMEM((SLOTS, B, B), bf16),
            pltpu.VMEM((ROUNDS, FP, B), jnp.int32),
            pltpu.VMEM((TABLE, B), jnp.int32),
            pltpu.SMEM((TABLE, B), jnp.int32),
            pltpu.VMEM((SLOTS, B, B), bf16),
            pltpu.VMEM((TABLE, B), jnp.int32),
            pltpu.SMEM((TABLE, B), jnp.int32),
            pltpu.VMEM((VOX, F, B), f32),
            pltpu.VMEM((FP, B), bf16),
            pltpu.VMEM((FP, B), bf16),
            pltpu.VMEM((NZ, FP, B), bf16),
        ]
        + [half] * (2 * ROUNDS)
        + [
            pltpu.VMEM((LENT, HALVES, VOX, F, B), bf16),
            pltpu.VMEM((HALVES, VOX, F, B), bf16),
            pltpu.VMEM((HALVES, VOX, F, B), bf16),
            pltpu.VMEM((SLOTS + 1, F, B), f32),
            pltpu.VMEM((SLOTS + 1, F, B), f32),
            pltpu.VMEM((SLOTS + 1, F, B), f32),
            pltpu.VMEM((VOX, F, B), f32),
            pltpu.VMEM((HALVES, OWN, F, B), bf16),
            pltpu.VMEM((HALVES, OWN, F, B), bf16),
            pltpu.VMEM((HALVES, OWN, F, B), bf16),
            pltpu.VMEM((HALVES, NY - 1, NZ, F, B), bf16),
            pltpu.VMEM((2, HALVES, NZ, F, B), bf16),
            pltpu.VMEM((2, HALVES, NZ - 1, NZ, F, B), bf16),
            pltpu.VMEM((RAYS, F, B), bf16),
            pltpu.VMEM((RAYS, F, B), bf16),
            pltpu.VMEM((NZ, len(OWN_ROUNDS), FP, B), bf16),
            dma((HALVES,)), dma((HALVES,)),
            dma((HALVES,)), dma((HALVES,)),
            dma((2, HALVES)), dma((2, HALVES)),
            dma((HALVES,)), dma((HALVES,)),
            dma((HALVES,)), dma((HALVES,)),
            dma((LENT, HALVES)), dma((LENT, HALVES)),
            dma((LENT, HALVES)), dma((LENT, HALVES)),
            dma, dma,
            dma((5,)), dma, dma((PARTS,)), dma((ROUNDS,)), dma((2,)),
            dma, dma, dma, dma, dma, dma, dma, dma,
        ],
        compiler_params=pltpu.CompilerParams(collective_id=0, has_side_effects=True, vmem_limit_bytes=56000000),
        name="fused",
    )(images, system_tiles, tile_vox, tile_ray, live_blocks, counts)


def solution(mesh):
    in_specs = (
        P("subset", "tile"),
        P("subset", "tile", None, None),
        P("subset", "tile"),
        P("subset", "tile"),
        P("subset", "tile"),
        P("subset", None, "tile"),
    )
    out_specs = P("subset", "tile")
    return jax.shard_map(shards, mesh=mesh, in_specs=in_specs, out_specs=out_specs, check_vma=False)
```

```python
import functools

import jax
import jax.numpy as jnp
from jax import lax
from jax.experimental import pallas as pl
from jax.experimental.pallas import tpu as pltpu
from jax.sharding import PartitionSpec as P

TILE_GROUP = 32
ROUNDS = 4
SUBSETS = 8
SLOTS = 32
VOX = 16
RAYS = 64
B = 128
NY = 8
NZ = 4
FP = 32
HALVES = 2
F = FP // HALVES
OWN = RAYS // 2
PARTS = 4
PIECES = 8
LENT = 2
OWN_ROUNDS = (0, 1, 3)

PREV_R, PREV_V, LAST_R, LAST_V, PLACE, VOX_OF, TABLE = 0, 1, 2, 3, 4, 5, 8

f32 = jnp.float32
bf16 = jnp.bfloat16


def fused(
    images_hbm, tiles_hbm, vox_hbm, ray_hbm, live_hbm, counts_hbm, out,
    vox_of, ray_of, live, vox_row, ray_row, images, own_tiles, counts, table_rows, own_table,
    lent_tiles, lent_rows, lent_table, lent_inverse, count_out, count_in, lent_cnt,
    low_0a, low_0b, low_1a, low_1b, low_2a, low_2b, low_3a, low_3b,
    rest, send_high, send_low, acc_a, acc_b, acc_back, own_inverse,
    send_c, recv_c, send_y, recv_y, send_z, recv_z, ratio_a, ratio_b, cnt,
    s_c, r_c, s_y, r_y, s_z, r_z, s_g, r_g, s_p, r_p, s_h, r_h, s_l, r_l, s_n, r_n,
    s_index, s_images, s_tiles, s_counts, s_table,
    s_t, r_t, s_i, r_i, s_k, r_k, s_m, r_m,
):
    low = ((low_0a, low_0b), (low_1a, low_1b), (low_2a, low_2b), (low_3a, low_3b))
    acc = (acc_a, acc_b)
    ratio = (ratio_a, ratio_b)
    subset = lax.axis_index("subset")
    tile = lax.axis_index("tile")
    core = lax.rem(tile, 2)
    z = lax.rem(lax.div(tile, 2), NZ)
    y = lax.div(tile, 2 * NZ)

    def at(y_of, z_of, c_of):
        return {"tile": (y_of * NZ + z_of) * 2 + c_of}

    partner = at(y, z, 1 - core)
    y_of = [None] + [lax.rem(y + k, NY) for k in range(1, NY)]
    y_peers = [None] + [at(y_of[k], z, core) for k in range(1, NY)]
    z_peers = [None] + [at(y, lax.rem(z + k, NZ), core) for k in range(1, NZ)]
    ahead = {"subset": lax.rem(subset + 1, SUBSETS)}
    behind = {"subset": lax.rem(subset + SUBSETS - 1, SUBSETS)}
    ahead_two = {"subset": lax.rem(subset + 2, SUBSETS)}
    behind_two = {"subset": lax.rem(subset + SUBSETS - 2, SUBSETS)}
    everyone = [partner] + y_peers[1:] + z_peers[1:] + [ahead, behind, ahead_two, behind_two]
    far_first_y = (4, 3, 5, 2, 6, 1, 7)
    far_first_z = (2, 1, 3)

    barrier = pltpu.get_barrier_semaphore()
    for peer in everyone:
        pl.semaphore_signal(barrier, inc=1, device_id=peer, device_id_type=pl.DeviceIdType.MESH)

    def remote(src, dst, send, recv, peer):
        return pltpu.make_async_remote_copy(
            src_ref=src, dst_ref=dst, send_sem=send, recv_sem=recv,
            device_id=peer, device_id_type=pl.DeviceIdType.MESH,
        )

    def await_bytes(ref, sem):
        pltpu.make_async_copy(ref, ref, sem).wait()

    def frames(h):
        return slice(h * F, (h + 1) * F)

    indices = [
        pltpu.make_async_copy(src, dst, s_index.at[i])
        for i, (src, dst) in enumerate(
            ((vox_hbm, vox_of), (ray_hbm, ray_of), (live_hbm, live), (vox_hbm, vox_row), (ray_hbm, ray_row))
        )
    ]
    for copy in indices:
        copy.start()
    copies = [pltpu.make_async_copy(images_hbm, images, s_images)]
    for i in range(PARTS):
        part = pl.ds(i * SLOTS // PARTS, SLOTS // PARTS)
        copies.append(pltpu.make_async_copy(tiles_hbm.at[0, part], own_tiles.at[part], s_tiles.at[i]))
    for r in range(ROUNDS):
        panel = lax.rem(subset - r + SUBSETS, SUBSETS)
        rows = pl.ds(pl.multiple_of(panel * FP, FP), FP)
        copies.append(pltpu.make_async_copy(counts_hbm.at[0, rows], counts.at[r], s_counts.at[r]))
    for copy in copies:
        copy.start()
    for copy in indices:
        copy.wait()

    slot = lax.broadcasted_iota(jnp.int32, (SLOTS, SLOTS), 0)
    later = lax.broadcasted_iota(jnp.int32, (SLOTS, SLOTS), 1)

    def latest(found):
        best = jnp.max(jnp.where(found, lax.broadcasted_iota(jnp.int32, found.shape, 0), -1), axis=0, keepdims=True)
        return jnp.where(best < 0, SLOTS, best)

    for block_of, row, prev, last, blocks in (
        (ray_of, ray_row, PREV_R, LAST_R, RAYS),
        (vox_of, vox_row, PREV_V, LAST_V, VOX),
    ):
        column = jnp.zeros((SLOTS, B), jnp.int32)
        which = lax.broadcasted_iota(jnp.int32, (SLOTS, B), 0)
        for t in range(SLOTS):
            column = jnp.where(which == t, block_of[0, t], column)
        column = jnp.where(which // TILE_GROUP < live[0, 0], column, -1)
        same = column[:, :SLOTS] == jnp.broadcast_to(row[...], (SLOTS, SLOTS))
        table_rows[prev : prev + 1, :SLOTS] = latest(same & (slot < later))
        block = lax.broadcasted_iota(jnp.int32, (SLOTS, B), 1)
        table_rows[last : last + 1, :] = latest(column == block)
    ray = ray_row[...]
    place = jnp.where(ray % 2 == core, 0, OWN) + ray // 2
    table_rows[PLACE : PLACE + 1, :SLOTS] = place
    table_rows[VOX_OF : VOX_OF + 1, :SLOTS] = vox_row[...]
    table_copy = pltpu.make_async_copy(table_rows, own_table, s_table.at[0])
    table_copy.start()

    for h in range(HALVES):
        acc[h][SLOTS] = jnp.zeros((F, B), f32)
    acc_back[SLOTS] = jnp.zeros((F, B), f32)
    copies[0].wait()
    for h in range(HALVES):
        for v in range(VOX):
            low[0][h][v] = images[frames(h), v * B : (v + 1) * B].astype(bf16)
    table_copy.wait()

    def with_tiles(r):
        return (lent_tiles, lent_table, lent_inverse) if r == LENT else (own_tiles, own_table, own_inverse)

    def project(r, h):
        tiles, table, _ = with_tiles(r)
        for t in range(0, SLOTS, 2):
            if r == 0 and h == 0 and t % (SLOTS // PARTS) == 0:
                copies[1 + t // (SLOTS // PARTS)].wait()
            chosen = jnp.concatenate([low[r][h][table[VOX_OF, t + i]] for i in range(2)], axis=0)
            pair = tiles[t : t + 2].reshape(2 * B, B)
            product = lax.dot_general(
                chosen, pair, (((1,), (1,)), ((), ())), preferred_element_type=f32
            )
            for i in range(2):
                mine = product[i * F : (i + 1) * F, i * B : (i + 1) * B]
                acc[h][t + i] = mine + acc[h][table[PREV_R, t + i]]
        for j in range(OWN):
            send_c[h, j] = acc[h][table[LAST_R, 2 * j + 1 - core]].astype(bf16)

    def backproject(r, h):
        tiles, table, _ = with_tiles(r)
        for t in range(0, SLOTS, 2):
            chosen = jnp.concatenate([ratio[h][table[PLACE, t + i]] for i in range(2)], axis=0)
            pair = jnp.concatenate([tiles[t], tiles[t + 1]], axis=1)
            product = jnp.dot(chosen, pair, preferred_element_type=f32)
            for i in range(2):
                mine = product[i * F : (i + 1) * F, i * B : (i + 1) * B]
                acc_back[t + i] = mine + acc_back[table[PREV_V, t + i]]

    def stage_c(r, h):
        if 0 < r <= LENT:
            await_bytes(low[r][h], r_h.at[r - 1, h])
        if r > 0:
            await_bytes(send_c.at[h], s_c.at[h])
        project(r, h)
        if r == 0 and h == 0:
            pl.semaphore_wait(barrier, len(everyone))
        remote(send_c.at[h], recv_c.at[h], s_c.at[h], r_c.at[h], partner).start()

    def stage_y(r, h):
        table = with_tiles(r)[1]
        await_bytes(recv_c.at[h], r_c.at[h])
        if r > 0:
            await_bytes(recv_y.at[h], s_y.at[h])
            await_bytes(ratio[h].at[pl.ds(0, OWN)], s_p.at[h])
        for j in range(OWN):
            own = acc[h][table[LAST_R, 2 * j + core]]
            send_y[h, j] = (own + recv_c[h, j].astype(f32)).astype(bf16)
        for k in far_first_y:
            remote(
                send_y.at[h, pl.ds(y_of[k] * NZ, NZ)], recv_y.at[h, k - 1],
                s_y.at[h], r_y.at[h], y_peers[k],
            ).start()

    def stage_z(r, h):
        p = r % 2
        await_bytes(recv_y.at[h], r_y.at[h])
        if r > 1:
            await_bytes(recv_z.at[p, h], s_z.at[p, h])
        for b in range(NZ):
            total = send_y[h, y * NZ + b].astype(f32)
            for k in range(NY - 1):
                total = total + recv_y[h, k, b].astype(f32)
            send_z[p, h, b] = total.astype(bf16)
        for k in far_first_z:
            remote(
                send_z.at[p, h], recv_z.at[p, h, k - 1], s_z.at[p, h], r_z.at[p, h], z_peers[k]
            ).start()

    def stage_g(r, h):
        p = r % 2
        await_bytes(recv_z.at[p, h], r_z.at[p, h])
        if r > 0:
            await_bytes(ratio[h].at[pl.ds(0, NZ * (NY - 1))], s_g.at[h])
        for b in range(NZ):
            even = send_z[p, h, b].astype(f32) + recv_z[p, h, 1, b].astype(f32)
            odd = recv_z[p, h, 0, b].astype(f32) + recv_z[p, h, 2, b].astype(f32)
            if r == LENT:
                measured = lent_cnt[b, frames(h), :].astype(f32)
            else:
                measured = cnt[b, OWN_ROUNDS.index(r), frames(h), :].astype(f32)
            ratio[h][y * NZ + b] = (measured / (even + odd)).astype(bf16)
        mine = ratio[h].at[pl.ds(y * NZ, NZ)]
        for k in far_first_y:
            remote(mine, mine, s_g.at[h], r_g.at[h], y_peers[k]).start()

    def stage_p(h):
        await_bytes(ratio[h].at[pl.ds(0, NZ * (NY - 1))], r_g.at[h])
        remote(
            ratio[h].at[pl.ds(0, OWN)], ratio[h].at[pl.ds(OWN, OWN)], s_p.at[h], r_p.at[h], partner
        ).start()

    def stage_b(r, h):
        last = r + 1 == ROUNDS
        _, table, inverse = with_tiles(r)
        await_bytes(ratio[h].at[pl.ds(OWN, OWN)], r_p.at[h])
        backproject(r, h)
        if 0 < r <= LENT:
            await_bytes(rest.at[r - 1, h], r_l.at[r - 1, h])
        if r == 1:
            await_bytes(send_high.at[h], s_h.at[r - 1, h])
            await_bytes(send_low.at[h], s_l.at[r - 1, h])
        for v in range(VOX):
            if r == 0:
                held = images[frames(h), v * B : (v + 1) * B]
            elif r <= LENT:
                held = low[r][h][v].astype(f32) + rest[r - 1, h, v].astype(f32)
            else:
                held = out[frames(h), v * B : (v + 1) * B]
            held = held * acc_back[table[LAST_V, v]] * inverse[v]
            if r >= LENT:
                out[frames(h), v * B : (v + 1) * B] = held
                if not last:
                    low[r + 1][h][v] = held.astype(bf16)
            else:
                high = held.astype(bf16)
                send_high[h, v] = high
                send_low[h, v] = (held - high.astype(f32)).astype(bf16)
        if r < LENT:
            target = ahead if r == 0 else ahead_two
            remote(send_high.at[h], low[r + 1][h], s_h.at[r, h], r_h.at[r, h], target).start()
            remote(send_low.at[h], rest.at[r, h], s_l.at[r, h], r_l.at[r, h], target).start()

    def sensitivity(r):
        tiles, table, inverse = with_tiles(r)
        ones = jnp.ones((F, B), bf16)
        for t in range(SLOTS):
            column = jnp.dot(ones, tiles[t], preferred_element_type=f32)
            acc_back[t] = column + acc_back[table[PREV_V, t]]
        for v in range(VOX):
            inverse[v] = 1.0 / acc_back[table[LAST_V, v]]

    def lend(i):
        for t in range(i * SLOTS // PIECES, (i + 1) * SLOTS // PIECES):
            remote(own_tiles.at[t], lent_tiles.at[t], s_t, r_t, ahead).start()

    def share_counts():
        for k in far_first_z:
            remote(cnt.at[z], cnt.at[z], s_n, r_n, z_peers[k]).start()
        remote(count_out, count_in, s_k, r_k, ahead).start()
        remote(table_rows, lent_rows, s_i, r_i, ahead).start()

    def take_lent():
        await_bytes(count_in, r_k)
        lent_cnt[z] = count_in[...]
        for k in far_first_z:
            remote(lent_cnt.at[z], lent_cnt.at[z], s_m, r_m, z_peers[k]).start()
        await_bytes(lent_rows, r_i)
        lent_copy = pltpu.make_async_copy(lent_rows, lent_table, s_table.at[1])
        lent_copy.start()
        lent_copy.wait()

    for i in range(ROUNDS):
        copies[1 + PARTS + i].wait()
        measured = counts[i].astype(f32).astype(bf16)
        if i == LENT:
            count_out[...] = measured
        else:
            cnt[z, OWN_ROUNDS.index(i)] = measured

    for r in range(ROUNDS):
        stage_c(r, 0)
        if r == 0:
            share_counts()
        if r == LENT + 1:
            stage_p(1)
        stage_y(r, 0)
        if r == LENT + 1:
            stage_b(LENT, 1)
        if r < LENT:
            lend(4 * r)
        stage_c(r, 1)
        stage_y(r, 1)
        if r < LENT:
            lend(4 * r + 1)
        if r in (0, LENT):
            sensitivity(r)
        stage_z(r, 0)
        stage_z(r, 1)
        if r == 0:
            await_bytes(cnt.at[pl.ds(0, NZ - 1)], r_n)
        if r == LENT:
            await_bytes(lent_cnt.at[pl.ds(0, NZ - 1)], r_m)
        stage_g(r, 0)
        stage_g(r, 1)
        if r < LENT:
            lend(4 * r + 2)
            lend(4 * r + 3)
        if r + 1 == LENT:
            take_lent()
        stage_p(0)
        stage_b(r, 0)
        if r != LENT:
            stage_p(1)
            stage_b(r, 1)
        if r + 1 == LENT:
            await_bytes(lent_tiles, r_t)

    await_bytes(own_tiles, s_t)
    await_bytes(table_rows, s_i)
    await_bytes(count_out, s_k)
    await_bytes(lent_cnt.at[pl.ds(0, NZ - 1)], s_m)
    await_bytes(cnt.at[pl.ds(0, NZ - 1)], s_n)
    for h in range(HALVES):
        await_bytes(send_c.at[h], s_c.at[h])
        await_bytes(recv_y.at[h], s_y.at[h])
        for p in range(2):
            await_bytes(recv_z.at[p, h], s_z.at[p, h])
        await_bytes(ratio[h].at[pl.ds(0, NZ * (NY - 1))], s_g.at[h])
        await_bytes(ratio[h].at[pl.ds(0, OWN)], s_p.at[h])
        await_bytes(send_high.at[h], s_h.at[LENT - 1, h])
        await_bytes(send_low.at[h], s_l.at[LENT - 1, h])


def shards(images, system_tiles, tile_vox, tile_ray, live_blocks, counts):
    hbm = pl.BlockSpec(memory_space=pl.ANY)
    half = pltpu.VMEM((VOX, F, B), bf16)
    dma = pltpu.SemaphoreType.DMA
    return pl.pallas_call(
        fused,
        out_shape=jax.ShapeDtypeStruct(images.shape, f32),
        in_specs=[hbm] * 6,
        out_specs=pl.BlockSpec(memory_space=pltpu.VMEM),
        scratch_shapes=[
            pltpu.SMEM((1, SLOTS), jnp.int32),
            pltpu.SMEM((1, SLOTS), jnp.int32),
            pltpu.SMEM((1, 1), jnp.int32),
            pltpu.VMEM((1, SLOTS), jnp.int32),
            pltpu.VMEM((1, SLOTS), jnp.int32),
            pltpu.VMEM((FP, VOX * B), f32),
            pltpu.VMEM((SLOTS, B, B), bf16),
            pltpu.VMEM((ROUNDS, FP, B), jnp.int32),
            pltpu.VMEM((TABLE, B), jnp.int32),
            pltpu.SMEM((TABLE, B), jnp.int32),
            pltpu.VMEM((SLOTS, B, B), bf16),
            pltpu.VMEM((TABLE, B), jnp.int32),
            pltpu.SMEM((TABLE, B), jnp.int32),
            pltpu.VMEM((VOX, F, B), f32),
            pltpu.VMEM((FP, B), bf16),
            pltpu.VMEM((FP, B), bf16),
            pltpu.VMEM((NZ, FP, B), bf16),
        ]
        + [half] * (2 * ROUNDS)
        + [
            pltpu.VMEM((LENT, HALVES, VOX, F, B), bf16),
            pltpu.VMEM((HALVES, VOX, F, B), bf16),
            pltpu.VMEM((HALVES, VOX, F, B), bf16),
            pltpu.VMEM((SLOTS + 1, F, B), f32),
            pltpu.VMEM((SLOTS + 1, F, B), f32),
            pltpu.VMEM((SLOTS + 1, F, B), f32),
            pltpu.VMEM((VOX, F, B), f32),
            pltpu.VMEM((HALVES, OWN, F, B), bf16),
            pltpu.VMEM((HALVES, OWN, F, B), bf16),
            pltpu.VMEM((HALVES, OWN, F, B), bf16),
            pltpu.VMEM((HALVES, NY - 1, NZ, F, B), bf16),
            pltpu.VMEM((2, HALVES, NZ, F, B), bf16),
            pltpu.VMEM((2, HALVES, NZ - 1, NZ, F, B), bf16),
            pltpu.VMEM((RAYS, F, B), bf16),
            pltpu.VMEM((RAYS, F, B), bf16),
            pltpu.VMEM((NZ, len(OWN_ROUNDS), FP, B), bf16),
            dma((HALVES,)), dma((HALVES,)),
            dma((HALVES,)), dma((HALVES,)),
            dma((2, HALVES)), dma((2, HALVES)),
            dma((HALVES,)), dma((HALVES,)),
            dma((HALVES,)), dma((HALVES,)),
            dma((LENT, HALVES)), dma((LENT, HALVES)),
            dma((LENT, HALVES)), dma((LENT, HALVES)),
            dma, dma,
            dma((5,)), dma, dma((PARTS,)), dma((ROUNDS,)), dma((2,)),
            dma, dma, dma, dma, dma, dma, dma, dma,
        ],
        compiler_params=pltpu.CompilerParams(collective_id=0, has_side_effects=True, vmem_limit_bytes=56000000),
        name="fused",
    )(images, system_tiles, tile_vox, tile_ray, live_blocks, counts)


def solution(mesh):
    in_specs = (
        P("subset", "tile"),
        P("subset", "tile", None, None),
        P("subset", "tile"),
        P("subset", "tile"),
        P("subset", "tile"),
        P("subset", None, "tile"),
    )
    out_specs = P("subset", "tile")
    return jax.shard_map(shards, mesh=mesh, in_specs=in_specs, out_specs=out_specs, check_vma=False)
```
